32 devices in a mesh: pb: 32 (over z, y, x, core).
Axes of the slice: x: 2, y: 2, z: 4, core: 2. Of those that a mesh axis runs over, the one named last changes fastest.
Arguments:
- densities: bfloat16 [32, 32, 32, 1200], P(None, 'pb'), may hold values from -1.1953125 to 1.1953125
- screening: bfloat16 [32, 1200, 1200], P('pb'), may hold values from -0.1875 to 0.1875
- live: int32 [32, 32], P(None, 'pb'), may hold values 0 or 1
Outputs:
- kernel: bfloat16 [32, 32, 256], P(None, 'pb')
The draws below stay inside these ranges and needn't reach their ends.
All inputs are finite; a program needn't handle non-finite values. No bound on the sum of `live` on one device may be relied on, other than what follows from the above.
Results may differ from the reference program's by a relative error of at most 0.0049.
Values may be sent and summed in bfloat16 or wider, within the bound.
No kernel may reach another device: no remote copies, remote signals or barrier semaphores. Data moves between devices by JAX's collectives and lax.ppermute only.
A program may use at most 128 MiB of HBM per device.

```python
import jax
import jax.numpy as jnp
from jax import lax

NG = 1200
PAIRS = 16
KROWS = 32
QS = 32


def plant(result, rng, smallest, high):
    place = [jax.random.randint(jax.random.fold_in(rng, axis), (), 0, length) for axis, length in enumerate(result.shape)]
    widest = result.shape.index(max(result.shape))
    next_to = place[:widest] + [(place[widest] + 1) % result.shape[widest]] + place[widest + 1:]
    return result.at[tuple(place)].set(smallest).at[tuple(next_to)].set(high)


def steps_of(key, dims, split, least, high):
    loudness = 1.0
    for position, parts in split:
        heights = jax.random.uniform(jax.random.fold_in(jax.random.fold_in(key, 6), position), (parts,), jnp.float32, least / len(split), high / len(split))
        loudness = loudness * jnp.repeat(jnp.exp(heights), dims[position] // parts).reshape((-1,) + (1,) * (len(dims) - 1 - position))
    return loudness


def gaussian(own_key, shape, deviation, most, pieces=(), held_as=jnp.bfloat16):
    gain = steps_of(own_key, shape, pieces, -0.22, 0.18) if pieces else 1.0
    array = jax.random.normal(own_key, shape, jnp.float32) * deviation * gain
    return jnp.minimum(jnp.maximum(array, -most), most).astype(held_as)


def setup_inputs(seed: int = 0) -> dict:
    keys = jax.random.split(jax.random.key(seed), 4)
    return {
        "densities": gaussian(keys[0], (QS, KROWS, 2 * PAIRS, NG), 0.2, 1.1953125, ((1, 32),)),
        "screening": gaussian(keys[1], (QS, NG, NG), NG ** -0.5, 0.1875, ((0, 32),)),
        "live": plant((jax.random.randint(keys[2], (QS, KROWS), 0, 4) < 3).astype(jnp.int32), jax.random.fold_in(keys[2], 1), 0, 1),
    }


def one_q(args):
    rho, weights, mask = args
    pairs = rho.shape[1] // 2
    valence = rho[:, pairs:, :].reshape(-1, rho.shape[2])
    screened = jnp.dot(valence, weights.T, preferred_element_type=jnp.float32).astype(jnp.bfloat16)
    screened = screened.reshape(rho.shape[0], pairs, rho.shape[2])
    blocks = jnp.einsum("kag,kbg->kab", rho[:, :pairs, :].astype(jnp.float32), screened.astype(jnp.float32))
    blocks = blocks.reshape(rho.shape[0], pairs * pairs) * mask.astype(jnp.float32)[:, None]
    return blocks.astype(jnp.bfloat16)


def reference(densities, screening, live):
    return lax.map(one_q, (densities, screening, live))
```

```python
import jax
import jax.numpy as jnp
from jax import lax
from jax.experimental import pallas as pl
from jax.experimental.pallas import tpu as pltpu
from jax.sharding import PartitionSpec as P


BF16, F32 = jnp.bfloat16, jnp.float32
LANES = 128
HALF = LANES // 2
COLS = 256


class Sizes:
    def __init__(self, shape, devices):
        self.q, _, both, self.ng = shape
        self.pairs = both // 2
        self.full, self.tail = divmod(self.ng, LANES)
        self.rows = self.pairs * self.full + (self.pairs // 2 if self.tail else 0)
        self.wide = LANES * (self.full + (1 if self.tail else 0))
        self.devices = devices
        bits = devices.bit_length() - 1
        self.outer = 2 ** (bits // 2)
        self.inner = devices // self.outer

    def fits(self):
        power = self.devices & (self.devices - 1) == 0
        return power and self.inner >= 4 and self.pairs == 16 and 0 < self.tail <= HALF


def call(kernel, outs, ins, specs, scratch=(), flops=0, moved=0, name=None):
    return pl.pallas_call(
        kernel,
        out_shape=tuple(outs),
        in_specs=specs,
        out_specs=tuple(pl.BlockSpec(memory_space=pltpu.VMEM) for _ in outs),
        scratch_shapes=list(scratch),
        compiler_params=pltpu.CompilerParams(vmem_limit_bytes=24 << 20),
        cost_estimate=pl.CostEstimate(flops=flops, bytes_accessed=moved, transcendentals=0),
        name=name,
    )(*ins)


VM = pl.BlockSpec(memory_space=pltpu.VMEM)
ANY = pl.BlockSpec(memory_space=pl.ANY)


def pack(s, read, dst, b, base):
    n = s.pairs
    for j in range(s.full):
        dst[b, base + n * j : base + n * (j + 1), :] = read(LANES * j, LANES * (j + 1))
    last = read(LANES * s.full, s.wide).astype(F32)
    lane = lax.broadcasted_iota(jnp.int32, (n // 2, LANES), 1)
    folded = jnp.where(lane < HALF, last[: n // 2], pltpu.roll(last[n // 2 :], HALF, 1))
    dst[b, base + n * s.full : base + s.rows, :] = folded.astype(BF16)


def unpack(s, src, b, base, dst, row):
    n = s.pairs
    for j in range(s.full):
        dst[row : row + n, LANES * j : LANES * (j + 1)] = src[b, base + n * j : base + n * (j + 1), :]
    folded = src[b, base + n * s.full : base + s.rows, :].astype(F32)
    last = jnp.concatenate([folded, pltpu.roll(folded, HALF, 1)], axis=0).astype(BF16)
    dst[row : row + n, LANES * s.full : s.ng] = last[:, : s.tail]


def nt(x, y):
    return lax.dot_general(x, y, (((1,), (1,)), ((), ())), preferred_element_type=F32)


def screen(s, v, w_ref, out):
    for lo in range(0, s.ng, COLS):
        hi = min(lo + COLS, s.ng)
        out[:, lo:hi] = nt(v[...], w_ref[0, lo:hi, :]).astype(BF16)


def rows_of_pairs(s, me, offsets, c, sc):
    n, count = s.pairs, len(offsets) * s.pairs
    full = nt(c, sc)
    r = lax.broadcasted_iota(jnp.int32, (count, count), 0)
    k = lax.broadcasted_iota(jnp.int32, (count, count), 1)
    own = jnp.where(r // n == k // n, full, 0.0).astype(BF16)
    e = lax.broadcasted_iota(jnp.int32, (count, n * n), 0)
    f = lax.broadcasted_iota(jnp.int32, (count, n * n), 1)
    spread = jnp.where(e % n == f % n, 1.0, 0.0).astype(BF16)
    x = jnp.dot(own, spread, preferred_element_type=F32)
    x = jnp.where(f // n == e % n, x, 0.0).astype(BF16)
    i = lax.broadcasted_iota(jnp.int32, (s.devices, count), 1) // n
    at = lax.broadcasted_iota(jnp.int32, (s.devices, count), 0)
    target = jnp.zeros_like(i)
    for index, m in enumerate(offsets):
        target = jnp.where(i == index, m, target)
    place = jnp.where(at == (target ^ me), 1.0, 0.0).astype(BF16)
    return jnp.dot(place, x, preferred_element_type=F32)


def gather(s, me, dens, offsets, half, buf, sem):
    lo, n = (0, 2 * s.pairs) if half is None else (half * s.pairs, s.pairs)
    copies = [
        pltpu.make_async_copy(dens.at[me ^ m, 0, pl.ds(lo, n), :], buf.at[i], sem.at[i])
        for i, m in enumerate(offsets)
    ]
    for c in copies:
        c.start()
    return copies


def reader(s, buf, i, row, edge):
    def read(lo, hi):
        if hi <= s.ng:
            return buf[i, row : row + s.pairs, lo:hi]
        edge[i, :, : s.tail] = buf[i, row : row + s.pairs, lo : s.ng]
        return edge[i]

    return read


def fast(s, densities, weights, live):
    me_arr = lax.axis_index("pb").astype(jnp.int32).reshape(1)
    SM = pl.BlockSpec(memory_space=pltpu.SMEM)
    O, I, N, n = s.outer, s.inner, s.devices, s.pairs
    inner = sorted(range(I), key=lambda p: (bin(p).count("1"), p))
    back, there = inner[: I // 2], inner[I // 2 :]
    groups = [there[: len(there) // 2], there[len(there) // 2 :]]
    h = len(back)
    far = list(range(O - 1, 0, -1))
    block = n * s.ng

    def sds(*shape):
        return jax.ShapeDtypeStruct(shape, BF16)

    def hop(x, m):
        return lax.ppermute(x, "pb", [(d, d ^ m) for d in range(N)])

    def take_v(me_ref, dens, *refs):
        outs, (buf, edge, sem) = refs[:O], refs[O:]
        me = me_ref[0]
        offs = [dz * I + p for dz in [*far, 0] for p in back]
        copies = gather(s, me, dens, offs, 1, buf, sem)
        for i, c in enumerate(copies):
            c.wait()
            dz, j = offs[i] // I, i % h
            pack(s, reader(s, buf, i, 0, edge), outs[dz], j, 0)

    vb = call(
        take_v,
        [sds(h, s.rows, LANES)] * O,
        (me_arr, densities),
        [SM, ANY],
        [pltpu.VMEM((O * h, n, s.ng), BF16), pltpu.VMEM((O * h, n, LANES), BF16), pltpu.SemaphoreType.DMA((O * h,))],
        moved=4 * O * h * block,
        name="take_v",
    )
    vz = {dz: hop(vb[dz], dz * I) for dz in far}

    def take_cv(group):
        g = len(group)

        def kernel(me_ref, dens, *refs):
            outs, (buf, edge, edge2, sem) = refs[:g], refs[g:]
            me = me_ref[0]
            offs = [dz * I + p for p in group for dz in range(O)]
            copies = gather(s, me, dens, offs, None, buf, sem)
            for i, c in enumerate(copies):
                c.wait()
                pack(s, reader(s, buf, i, 0, edge), outs[i // O], i % O, 0)
                pack(s, reader(s, buf, i, n, edge2), outs[i // O], i % O, s.rows)

        k = O * g
        return call(
            kernel,
            [sds(O, 2 * s.rows, LANES)] * g,
            (me_arr, densities),
            [SM, ANY],
            [
                pltpu.VMEM((k, 2 * n, s.ng), BF16),
                pltpu.VMEM((k, n, LANES), BF16),
                pltpu.VMEM((k, n, LANES), BF16),
                pltpu.SemaphoreType.DMA((k,)),
            ],
            moved=8 * k * block,
            name="take_cv",
        )

    def regroup(name, picks, count, parts, ins):
        def kernel(*refs):
            src, outs = refs[: len(ins)], refs[len(ins) :]
            for o, pick in zip(outs, picks):
                for i, (a, b) in enumerate(pick):
                    o[i] = src[a][b]

        return call(
            kernel,
            [sds(count, parts * s.rows, LANES)] * len(picks),
            ins,
            [VM] * len(ins),
            moved=4 * len(picks) * count * parts * block,
            name=name,
        )

    arrived = []
    for group in groups:
        sent = take_cv(group)
        near = [hop(x, p) for x, p in zip(sent, group)]
        g = len(group)
        parts = regroup(
            "onward", [[(j, dz) for j in range(g)] for dz in [0, *far]], g, 2, near
        )
        arrived.append([(0, parts[0])] + [(dz, hop(x, dz * I)) for dz, x in zip(far, parts[1:])])

    zs = [vb[0]] + [vz[dz] for dz in far]
    order = [0, *far]
    pieces = regroup("inward", [[(a, j) for a in range(O)] for j in range(h)], O, 1, zs)
    own_v, send_v = pieces[0], pieces[1:]
    vin = [own_v] + [hop(x, p) for x, p in zip(send_v, back[1:])]

    def screen_back(*refs):
        src, w_ref, outs, (v, sc) = refs[:h], refs[h], refs[h + 1 : 2 * h + 1], refs[2 * h + 1 :]
        for j in range(h):
            for a in range(O):
                unpack(s, src[j], a, 0, v, n * (j * O + a))
        screen(s, v, w_ref, sc)
        for j in range(h):
            for a in range(O):
                row = n * (j * O + a)
                pack(s, lambda lo, hi, row=row: sc[row : row + n, lo:hi], outs[j], a, 0)

    m_rows = n * h * O
    sb = call(
        screen_back,
        [sds(O, s.rows, LANES)] * h,
        (*vin, weights),
        [VM] * (h + 1),
        [pltpu.VMEM((m_rows, s.ng), BF16), pltpu.VMEM((m_rows, s.wide), BF16)],
        flops=2 * m_rows * s.ng * s.ng,
        moved=2 * s.ng * s.ng,
        name="screen_back",
    )
    sin = [sb[0]] + [hop(x, p) for x, p in zip(sb[1:], back[1:])]
    out_z = regroup("outward", [[(j, a) for j in range(h)] for a in range(O)], h, 1, sin)
    sz = [out_z[0]] + [hop(x, dz * I) for dz, x in zip(far, out_z[1:])]

    def blocks_at_owner(group, index, prior):
        g = len(group)
        got = arrived[index]
        offs = [dz * I + p for dz, _ in got for p in group]
        count = len(offs)
        last = prior is not None

        def kernel(me_ref, *refs):
            src, w_ref = refs[:O], refs[O]
            rest = refs[O + 1 :]
            if last:
                before, rest = rest[0], rest[1:]
            out, c, v, sc = rest
            for a in range(O):
                for j in range(g):
                    unpack(s, src[a], j, 0, c, n * (a * g + j))
                    unpack(s, src[a], j, s.rows, v, n * (a * g + j))
            screen(s, v, w_ref, sc)
            r = rows_of_pairs(s, me_ref[0], offs, c[...], sc[:, : s.ng])
            if last:
                r = r + before[...]
                for t in range(n * n // LANES):
                    out[:, t, :] = r[:, LANES * t : LANES * (t + 1)].astype(BF16)
            else:
                out[...] = r

        shape = (N, n * n // LANES, LANES) if last else (N, n * n)
        return call(
            kernel,
            [jax.ShapeDtypeStruct(shape, BF16 if last else F32)],
            (me_arr, *[x for _, x in got], weights) + ((prior,) if last else ()),
            [SM] + [VM] * (O + 1 + (1 if last else 0)),
            [
                pltpu.VMEM((n * count, s.ng), BF16),
                pltpu.VMEM((n * count, s.ng), BF16),
                pltpu.VMEM((n * count, s.wide), BF16),
            ],
            flops=2 * n * count * s.ng * s.ng,
            moved=2 * s.ng * s.ng,
            name="blocks_at_owner",
        )[0]

    sums = None
    for index, group in enumerate(groups):
        sums = blocks_at_owner(group, index, sums)
    returned = lax.all_to_all(sums, "pb", split_axis=0, concat_axis=0, tiled=True)

    offs_c = [dz * I + p for dz in order for p in back]

    def take_c(me_ref, dens, out, sem):
        for c in gather(s, me_ref[0], dens, offs_c, 0, out, sem):
            c.wait()

    own_c = call(
        take_c,
        [sds(len(offs_c), n, s.ng)],
        (me_arr, densities),
        [SM, ANY],
        [pltpu.SemaphoreType.DMA((len(offs_c),))],
        moved=4 * len(offs_c) * block,
        name="take_c",
    )[0]

    def finish(me_ref, c_ref, live_ref, back_ref, *refs):
        src, out, c, sc = refs[:O], refs[O], refs[O + 1], refs[O + 2]
        for a in range(O):
            for j in range(h):
                row = n * (a * h + j)
                c[row : row + n, :] = c_ref[a * h + j]
                unpack(s, src[a], j, 0, sc, row)
        r = jnp.concatenate([back_ref[:, t, :].astype(F32) for t in range(n * n // LANES)], axis=1)
        half = O // 2 * h * n
        for lo in (0, half):
            r = r + rows_of_pairs(s, me_ref[0], offs_c[lo // n : lo // n + half // n], c[lo : lo + half, :], sc[lo : lo + half, :])
        out[...] = (r * live_ref[...].astype(F32)).astype(BF16)

    out = call(
        finish,
        [sds(N, n * n)],
        (me_arr, own_c, live, returned, *sz),
        [SM] + [VM] * (3 + O),
        [pltpu.VMEM((m_rows, s.ng), BF16), pltpu.VMEM((m_rows, s.ng), BF16)],
        flops=2 * m_rows * s.ng * n,
        moved=4 * m_rows * s.ng,
        name="finish",
    )[0]
    return out[:, None, :]


def plain(densities, screening, live):
    pairs = densities.shape[2] // 2
    arrived = lax.all_to_all(densities, "pb", split_axis=0, concat_axis=0, tiled=True)
    screened = jnp.einsum(
        "nkbh,gh->nkbg", arrived[:, :, pairs:, :], screening[0], preferred_element_type=F32
    ).astype(BF16)
    blocks = jnp.einsum("nkag,nkbg->nkab", arrived[:, :, :pairs, :], screened, preferred_element_type=F32)
    blocks = blocks.reshape(blocks.shape[0], blocks.shape[1], -1).astype(BF16)
    result = lax.all_to_all(blocks, "pb", split_axis=0, concat_axis=0, tiled=True)
    return result * live.astype(BF16)[:, :, None]


def solution(mesh):
    devices = mesh.shape["pb"]

    def on_device(densities, screening, live):
        s = Sizes(densities.shape, devices)
        if s.q == devices and s.fits():
            return fast(s, densities, screening, live)
        return plain(densities, screening, live)

    in_specs = (P(None, "pb", None, None), P("pb", None, None), P(None, "pb"))
    return jax.shard_map(
        on_device, mesh=mesh, in_specs=in_specs, out_specs=P(None, "pb", None), check_vma=False
    )
```

```python
import jax
import jax.numpy as jnp
from jax import lax
from jax.experimental import pallas as pl
from jax.experimental.pallas import tpu as pltpu
from jax.sharding import PartitionSpec as P


BF16, F32 = jnp.bfloat16, jnp.float32
LANES = 128
HALF = LANES // 2
COLS = 256


VM = pl.BlockSpec(memory_space=pltpu.VMEM)
SM = pl.BlockSpec(memory_space=pltpu.SMEM)
ANY = pl.BlockSpec(memory_space=pl.ANY)
HBM = pl.BlockSpec(memory_space=pltpu.HBM)


def split(devices):
    outer = 2 ** ((devices.bit_length() - 1) // 2)
    return outer, devices // outer


class Sizes:
    def __init__(self, shape, devices):
        self.q, _, both, self.ng = shape
        self.pairs = both // 2
        self.full, self.tail = divmod(self.ng, LANES)
        self.rows = self.pairs * self.full + (self.pairs // 2 if self.tail else 0)
        self.wide = LANES * (self.full + (1 if self.tail else 0))
        self.devices = devices
        self.outer, self.inner = split(devices)

    def fits(self):
        power = self.devices & (self.devices - 1) == 0
        return power and self.inner >= 4 and self.pairs == 16 and 0 < self.tail <= HALF


def call(kernel, outs, ins, specs, scratch=(), flops=0, moved=0, after=()):
    k, a = len(ins), len(after)

    def body(*refs):
        kernel(*refs[:k], *refs[k + a :])

    return pallas(body, outs, specs, a, scratch, flops, moved)(*ins, *after)


def pallas(body, outs, specs, a, scratch, flops, moved):
    return pl.pallas_call(
        body,
        out_shape=tuple(outs),
        in_specs=[*specs, *[ANY] * a],
        out_specs=tuple(pl.BlockSpec(memory_space=pltpu.VMEM) for _ in outs),
        scratch_shapes=list(scratch),
        compiler_params=pltpu.CompilerParams(vmem_limit_bytes=24 << 20),
        cost_estimate=pl.CostEstimate(flops=flops, bytes_accessed=moved, transcendentals=0),
    )


def pack(s, read, dst, b, base):
    n = s.pairs
    for j in range(s.full):
        dst[b, base + n * j : base + n * (j + 1), :] = read(LANES * j, LANES * (j + 1))
    last = read(LANES * s.full, s.wide).astype(F32)
    lane = lax.broadcasted_iota(jnp.int32, (n // 2, LANES), 1)
    folded = jnp.where(lane < HALF, last[: n // 2], pltpu.roll(last[n // 2 :], HALF, 1))
    dst[b, base + n * s.full : base + s.rows, :] = folded.astype(BF16)


def unpack(s, src, b, base, dst, row):
    n = s.pairs
    for j in range(s.full):
        dst[row : row + n, LANES * j : LANES * (j + 1)] = src[b, base + n * j : base + n * (j + 1), :]
    folded = src[b, base + n * s.full : base + s.rows, :].astype(F32)
    last = jnp.concatenate([folded, pltpu.roll(folded, HALF, 1)], axis=0).astype(BF16)
    dst[row : row + n, LANES * s.full : s.ng] = last[:, : s.tail]


def nt(x, y):
    return lax.dot_general(x, y, (((1,), (1,)), ((), ())), preferred_element_type=F32)


def screen(s, v, w_ref, out):
    for lo in range(0, s.ng, COLS):
        hi = min(lo + COLS, s.ng)
        out[:, lo:hi] = nt(v[...], w_ref[0, lo:hi, :]).astype(BF16)


def rows_of_pairs(s, me, offsets, c, sc):
    n, count = s.pairs, len(offsets) * s.pairs
    full = nt(c, sc)
    r = lax.broadcasted_iota(jnp.int32, (count, count), 0)
    k = lax.broadcasted_iota(jnp.int32, (count, count), 1)
    own = jnp.where(r // n == k // n, full, 0.0).astype(BF16)
    e = lax.broadcasted_iota(jnp.int32, (count, n * n), 0)
    f = lax.broadcasted_iota(jnp.int32, (count, n * n), 1)
    spread = jnp.where(e % n == f % n, 1.0, 0.0).astype(BF16)
    x = jnp.dot(own, spread, preferred_element_type=F32)
    x = jnp.where(f // n == e % n, x, 0.0).astype(BF16)
    i = lax.broadcasted_iota(jnp.int32, (s.devices, count), 1) // n
    at = lax.broadcasted_iota(jnp.int32, (s.devices, count), 0)
    target = jnp.zeros_like(i)
    for index, m in enumerate(offsets):
        target = jnp.where(i == index, m, target)
    place = jnp.where(at == (target ^ me), 1.0, 0.0).astype(BF16)
    return jnp.dot(place, x, preferred_element_type=F32)


def gather(s, me, dens, offsets, half, buf, sem):
    lo, n = (0, 2 * s.pairs) if half is None else (half * s.pairs, s.pairs)
    copies = [
        pltpu.make_async_copy(dens.at[me ^ m, 0, pl.ds(lo, n), :], buf.at[i], sem.at[i])
        for i, m in enumerate(offsets)
    ]
    for c in copies:
        c.start()
    return copies


def reader(s, buf, i, row, edge):
    def read(lo, hi):
        if hi <= s.ng:
            return buf[i, row : row + s.pairs, lo:hi]
        edge[i, :, : s.tail] = buf[i, row : row + s.pairs, lo : s.ng]
        return edge[i]

    return read


def fast(s, densities, weights, live):
    me_arr = lax.axis_index("pb").astype(jnp.int32).reshape(1)
    O, I, N, n = s.outer, s.inner, s.devices, s.pairs
    inner = sorted(range(I), key=lambda p: (bin(p).count("1"), p))
    back, there = inner[: I // 2], inner[I // 2 :]
    groups = [there[: len(there) // 2], there[len(there) // 2 :]]
    h = len(back)
    far = list(range(O - 1, 0, -1))
    block = n * s.ng

    def sds(*shape):
        return jax.ShapeDtypeStruct(shape, BF16)

    def hop(x, m):
        return lax.ppermute(x, "pb", [(d, d ^ m) for d in range(N)])

    densities = pltpu.with_memory_space_constraint(densities, pltpu.HBM)

    def take_v(me_ref, dens, *refs):
        outs, (buf, edge, sem) = refs[:O], refs[O:]
        me = me_ref[0]
        offs = [dz * I + p for dz in [*far, 0] for p in back]
        copies = gather(s, me, dens, offs, 1, buf, sem)
        for i, c in enumerate(copies):
            c.wait()
            dz, j = offs[i] // I, i % h
            pack(s, reader(s, buf, i, 0, edge), outs[dz], j, 0)

    vb = call(
        take_v,
        [sds(h, s.rows, LANES)] * O,
        (me_arr, densities),
        [SM, HBM],
        [pltpu.VMEM((O * h, n, s.ng), BF16), pltpu.VMEM((O * h, n, LANES), BF16), pltpu.SemaphoreType.DMA((O * h,))],
        moved=4 * O * h * block,
    )
    vz = {dz: hop(vb[dz], dz * I) for dz in far}

    def take_cv(index):
        group = groups[index]
        g = len(group)

        def kernel(me_ref, dens, *refs):
            outs, (buf, edge, edge2, sem) = refs[:g], refs[g:]
            me = me_ref[0]
            offs = [dz * I + p for p in group for dz in range(O)]
            copies = gather(s, me, dens, offs, None, buf, sem)
            for i, c in enumerate(copies):
                c.wait()
                pack(s, reader(s, buf, i, 0, edge), outs[i // O], i % O, 0)
                pack(s, reader(s, buf, i, n, edge2), outs[i // O], i % O, s.rows)

        k = O * g
        return call(
            kernel,
            [sds(O, 2 * s.rows, LANES)] * g,
            (me_arr, densities),
            [SM, HBM],
            [
                pltpu.VMEM((k, 2 * n, s.ng), BF16),
                pltpu.VMEM((k, n, LANES), BF16),
                pltpu.VMEM((k, n, LANES), BF16),
                pltpu.SemaphoreType.DMA((k,)),
            ],
            moved=8 * k * block,
            after=(vb[0],),
        )

    def regroup(picks, count, parts, ins, after=()):
        def kernel(*refs):
            src, outs = refs[: len(ins)], refs[len(ins) :]
            for o, pick in zip(outs, picks):
                for i, (a, b) in enumerate(pick):
                    o[i] = src[a][b]

        return call(
            kernel,
            [sds(count, parts * s.rows, LANES)] * len(picks),
            ins,
            [VM] * len(ins),
            moved=4 * len(picks) * count * parts * block,
            after=after,
        )

    early, late = [0, *range(1, O // 2)], list(range(O - 1, O // 2 - 1, -1))

    def take_c(me_ref, dens, *refs):
        outs, sems = refs[:2], refs[2]
        copies = []
        for t, zs in enumerate((early, late)):
            offs = [dz * I + p for dz in zs for p in back]
            copies += gather(s, me_ref[0], dens, offs, 0, outs[t], sems.at[t])
        for c in copies:
            c.wait()

    def onward(index, after):
        near, group = nears[index], groups[index]
        g = len(group)
        parts = regroup([[(j, dz) for j in range(g)] for dz in [0, *far]], g, 2, near, after)
        return [(0, parts[0])] + [(dz, hop(x, dz * I)) for dz, x in zip(far, parts[1:])]

    sents = [take_cv(index) for index in range(2)]
    nears = [[hop(x, p) for x, p in zip(sent, group)] for sent, group in zip(sents, groups)]
    own_c = call(
        take_c,
        [sds(O // 2 * h, n, s.ng)] * 2,
        (me_arr, densities),
        [SM, HBM],
        [pltpu.SemaphoreType.DMA((2, O // 2 * h))],
        moved=4 * O * h * block,
        after=(sents[1][0],),
    )
    arrived = [onward(0, (own_c[0],))]

    zs = [vb[0]] + [vz[dz] for dz in far]
    order = [0, *far]
    pieces = regroup([[(a, j) for a in range(O)] for j in range(h)], O, 1, zs, (arrived[0][0][1],))
    arrived.append(onward(1, (pieces[0],)))
    own_v, send_v = pieces[0], pieces[1:]
    vin = [own_v] + [hop(x, p) for x, p in zip(send_v, back[1:])]

    def screen_back(*refs):
        src, w_ref, outs, (v, sc) = refs[:h], refs[h], refs[h + 1 : 2 * h + 1], refs[2 * h + 1 :]
        for j in range(h):
            for a in range(O):
                unpack(s, src[j], a, 0, v, n * (j * O + a))
        screen(s, v, w_ref, sc)
        for j in range(h):
            for a in range(O):
                row = n * (j * O + a)
                pack(s, lambda lo, hi, row=row: sc[row : row + n, lo:hi], outs[j], a, 0)

    m_rows = n * h * O
    sb = call(
        screen_back,
        [sds(O, s.rows, LANES)] * h,
        (*vin, weights),
        [VM] * (h + 1),
        [pltpu.VMEM((m_rows, s.ng), BF16), pltpu.VMEM((m_rows, s.wide), BF16)],
        flops=2 * m_rows * s.ng * s.ng,
        moved=2 * s.ng * s.ng,
        after=(arrived[1][0][1],),
    )
    sin = [sb[0]] + [hop(x, p) for x, p in zip(sb[1:], back[1:])]
    out_z = regroup([[(j, a) for j in range(h)] for a in range(O)], h, 1, sin)
    sz = [out_z[0]] + [hop(x, dz * I) for dz, x in zip(far, out_z[1:])]

    def blocks_at_owner(group, index, prior):
        g = len(group)
        got = arrived[index]
        offs = [dz * I + p for dz, _ in got for p in group]
        count = len(offs)
        last = prior is not None

        def kernel(me_ref, *refs):
            src, w_ref = refs[:O], refs[O]
            rest = refs[O + 1 :]
            if last:
                before, rest = rest[0], rest[1:]
            out, c, v, sc = rest
            for a in range(O):
                for j in range(g):
                    unpack(s, src[a], j, 0, c, n * (a * g + j))
                    unpack(s, src[a], j, s.rows, v, n * (a * g + j))
            screen(s, v, w_ref, sc)
            r = rows_of_pairs(s, me_ref[0], offs, c[...], sc[:, : s.ng])
            if last:
                r = r + before[...]
                for t in range(n * n // LANES):
                    out[:, t, :] = r[:, LANES * t : LANES * (t + 1)].astype(BF16)
            else:
                out[...] = r

        shape = (N, n * n // LANES, LANES) if last else (N, n * n)
        return call(
            kernel,
            [jax.ShapeDtypeStruct(shape, BF16 if last else F32)],
            (me_arr, *[x for _, x in got], weights) + ((prior,) if last else ()),
            [SM] + [VM] * (O + 1 + (1 if last else 0)),
            [
                pltpu.VMEM((n * count, s.ng), BF16),
                pltpu.VMEM((n * count, s.ng), BF16),
                pltpu.VMEM((n * count, s.wide), BF16),
            ],
            flops=2 * n * count * s.ng * s.ng,
            moved=2 * s.ng * s.ng,
            after=(out_z[0],),
        )[0]

    sums = None
    for index, group in enumerate(groups):
        sums = blocks_at_owner(group, index, sums)
    returned = lax.all_to_all(sums, "pb", split_axis=0, concat_axis=0, tiled=True)

    def finish(part, zs, first):
        count = len(zs) * h
        offs = [dz * I + p for dz in zs for p in back]

        def kernel(me_ref, c_ref, *refs):
            src, (before, live_ref, out, c, sc) = refs[: len(zs)], refs[len(zs) :]
            for a in range(len(zs)):
                for j in range(h):
                    row = n * (a * h + j)
                    c[row : row + n, :] = c_ref[a * h + j]
                    unpack(s, src[a], j, 0, sc, row)
            r = rows_of_pairs(s, me_ref[0], offs, c[...], sc[...])
            if part == 0:
                r = r + jnp.concatenate([before[:, t, :].astype(F32) for t in range(n * n // LANES)], axis=1)
                out[...] = r
            else:
                out[...] = ((r + before[...]) * live_ref[...].astype(F32)).astype(BF16)

        return call(
            kernel,
            [jax.ShapeDtypeStruct((N, n * n), F32 if part == 0 else BF16)],
            (me_arr, own_c[part], *[sz[order.index(dz)] for dz in zs], first, live),
            [SM] + [VM] * (3 + len(zs)),
            [pltpu.VMEM((n * count, s.ng), BF16), pltpu.VMEM((n * count, s.ng), BF16)],
            flops=2 * n * count * s.ng * n,
            moved=4 * n * count * s.ng,
        )[0]

    return finish(1, late, finish(0, early, returned))[:, None, :]


def plain(densities, screening, live):
    pairs = densities.shape[2] // 2
    arrived = lax.all_to_all(densities, "pb", split_axis=0, concat_axis=0, tiled=True)
    screened = jnp.einsum(
        "nkbh,gh->nkbg", arrived[:, :, pairs:, :], screening[0], preferred_element_type=F32
    ).astype(BF16)
    blocks = jnp.einsum("nkag,nkbg->nkab", arrived[:, :, :pairs, :], screened, preferred_element_type=F32)
    blocks = blocks.reshape(blocks.shape[0], blocks.shape[1], -1).astype(BF16)
    result = lax.all_to_all(blocks, "pb", split_axis=0, concat_axis=0, tiled=True)
    return result * live.astype(BF16)[:, :, None]


def solution(mesh):
    devices = mesh.shape["pb"]

    def on_device(densities, screening, live):
        s = Sizes(densities.shape, devices)
        if s.q == devices and s.fits():
            return fast(s, densities, screening, live)
        return plain(densities, screening, live)

    in_specs = (P(None, "pb", None, None), P("pb", None, None), P(None, "pb"))
    return jax.shard_map(
        on_device, mesh=mesh, in_specs=in_specs, out_specs=P(None, "pb", None), check_vma=False
    )
```

```python
import jax
import jax.numpy as jnp
from jax import lax
from jax.experimental import pallas as pl
from jax.experimental.pallas import tpu as pltpu
from jax.sharding import PartitionSpec as P


BF16, F32 = jnp.bfloat16, jnp.float32
LANES = 128
HALF = LANES // 2
COLS = 256


VM = pl.BlockSpec(memory_space=pltpu.VMEM)
SM = pl.BlockSpec(memory_space=pltpu.SMEM)
ANY = pl.BlockSpec(memory_space=pl.ANY)
HBM = pl.BlockSpec(memory_space=pltpu.HBM)


def split(devices):
    outer = 2 ** ((devices.bit_length() - 1) // 2)
    return outer, devices // outer


class Sizes:
    def __init__(self, shape, devices):
        self.q, _, both, self.ng = shape
        self.pairs = both // 2
        self.full, self.tail = divmod(self.ng, LANES)
        self.rows = self.pairs * self.full + (self.pairs // 2 if self.tail else 0)
        self.wide = LANES * (self.full + (1 if self.tail else 0))
        self.devices = devices
        self.outer, self.inner = split(devices)

    def fits(self):
        power = self.devices & (self.devices - 1) == 0
        return power and self.inner >= 4 and self.pairs == 16 and 0 < self.tail <= HALF


def call(kernel, outs, ins, specs, scratch=(), flops=0, moved=0, after=()):
    k, a = len(ins), len(after)

    def body(*refs):
        kernel(*refs[:k], *refs[k + a :])

    return pallas(body, outs, specs, a, scratch, flops, moved)(*ins, *after)


def pallas(body, outs, specs, a, scratch, flops, moved):
    return pl.pallas_call(
        body,
        out_shape=tuple(outs),
        in_specs=[*specs, *[ANY] * a],
        out_specs=tuple(pl.BlockSpec(memory_space=pltpu.VMEM) for _ in outs),
        scratch_shapes=list(scratch),
        compiler_params=pltpu.CompilerParams(vmem_limit_bytes=24 << 20),
        cost_estimate=pl.CostEstimate(flops=flops, bytes_accessed=moved, transcendentals=0),
    )


def pack(s, read, dst, b, base):
    n = s.pairs
    for j in range(s.full):
        dst[b, base + n * j : base + n * (j + 1), :] = read(LANES * j, LANES * (j + 1))
    last = read(LANES * s.full, s.wide).astype(F32)
    lane = lax.broadcasted_iota(jnp.int32, (n // 2, LANES), 1)
    folded = jnp.where(lane < HALF, last[: n // 2], pltpu.roll(last[n // 2 :], HALF, 1))
    dst[b, base + n * s.full : base + s.rows, :] = folded.astype(BF16)


def unpack(s, src, b, base, dst, row):
    n = s.pairs
    src = src if b is None else src.at[b]
    for j in range(s.full):
        dst[row : row + n, LANES * j : LANES * (j + 1)] = src[base + n * j : base + n * (j + 1), :]
    folded = src[base + n * s.full : base + s.rows, :].astype(F32)
    last = jnp.concatenate([folded, pltpu.roll(folded, HALF, 1)], axis=0).astype(BF16)
    dst[row : row + n, LANES * s.full : s.ng] = last[:, : s.tail]


def nt(x, y):
    return lax.dot_general(x, y, (((1,), (1,)), ((), ())), preferred_element_type=F32)


def screen(s, v, w_ref, out):
    for lo in range(0, s.ng, COLS):
        hi = min(lo + COLS, s.ng)
        out[:, lo:hi] = nt(v[...], w_ref[0, lo:hi, :]).astype(BF16)


def spread(s, c, sc):
    n, count = s.pairs, c.shape[0]
    full = nt(c, sc)
    r = lax.broadcasted_iota(jnp.int32, (count, count), 0)
    k = lax.broadcasted_iota(jnp.int32, (count, count), 1)
    own = jnp.where(r // n == k // n, full, 0.0).astype(BF16)
    e = lax.broadcasted_iota(jnp.int32, (count, n * n), 0)
    f = lax.broadcasted_iota(jnp.int32, (count, n * n), 1)
    copies = jnp.where(e % n == f % n, 1.0, 0.0).astype(BF16)
    x = jnp.dot(own, copies, preferred_element_type=F32)
    return jnp.where(f // n == e % n, x, 0.0).astype(BF16)


def pick(shape, wanted):
    row = lax.broadcasted_iota(jnp.int32, shape, 0)
    column = lax.broadcasted_iota(jnp.int32, shape, 1)
    return jnp.where(wanted(row, column), 1.0, 0.0).astype(BF16)


def table(index, values):
    out = jnp.zeros_like(index)
    for i, value in enumerate(values):
        out = jnp.where(index == i, value, out)
    return out


def rows_of_pairs(s, me, offsets, c, sc):
    x = spread(s, c, sc)
    place = pick((s.devices, x.shape[0]), lambda q, r: q == (table(r // s.pairs, offsets) ^ me))
    return jnp.dot(place, x, preferred_element_type=F32)


def gather(s, me, dens, offsets, half, buf, sem):
    lo, n = (0, 2 * s.pairs) if half is None else (half * s.pairs, s.pairs)
    copies = [
        pltpu.make_async_copy(dens.at[me ^ m, 0, pl.ds(lo, n), :], buf.at[i], sem.at[i])
        for i, m in enumerate(offsets)
    ]
    for c in copies:
        c.start()
    return copies


def reader(s, buf, i, row, edge):
    def read(lo, hi):
        if hi <= s.ng:
            return buf[i, row : row + s.pairs, lo:hi]
        edge[i, :, : s.tail] = buf[i, row : row + s.pairs, lo : s.ng]
        return edge[i]

    return read


def parts_of(devices):
    outer, count = split(devices)
    inner = sorted(range(count), key=lambda p: (bin(p).count("1"), p))
    back, there = inner[: count // 2], inner[count // 2 :]
    half = len(there) // 2
    return [back[:half], back[half:]], [there[:half], there[half:]], list(range(outer - 1, 0, -1))


def fast(s, densities, weights, live):
    me_arr = lax.axis_index("pb").astype(jnp.int32).reshape(1)
    O, I, N, n = s.outer, s.inner, s.devices, s.pairs
    backs, groups, far = parts_of(N)
    order = [0, *far]
    back, there = backs[0] + backs[1], groups[0] + groups[1]
    h, g = len(back), len(groups[0])
    T = n * n // LANES
    block = n * s.ng

    def sds(*shape):
        return jax.ShapeDtypeStruct(shape, BF16)

    def hop(x, m):
        return lax.ppermute(x, "pb", [(d, d ^ m) for d in range(N)])

    densities = pltpu.with_memory_space_constraint(densities, pltpu.HBM)

    def take_v(zs, after):
        def kernel(me_ref, dens, *refs):
            outs, (buf, edge, sem) = refs[: len(zs)], refs[len(zs) :]
            offs = [dz * I + p for dz in zs for p in back]
            for i, c in enumerate(gather(s, me_ref[0], dens, offs, 1, buf, sem)):
                c.wait()
                pack(s, reader(s, buf, i, 0, edge), outs[i // h], i % h, 0)

        k = len(zs) * h
        return call(
            kernel,
            [sds(h, s.rows, LANES)] * len(zs),
            (me_arr, densities),
            [SM, HBM],
            [pltpu.VMEM((k, n, s.ng), BF16), pltpu.VMEM((k, n, LANES), BF16), pltpu.SemaphoreType.DMA((k,))],
            moved=4 * k * block,
            after=after,
        )

    first = take_v(far[:1], ())
    rest = take_v([*far[1:], 0], (first[0],))
    vb = dict(zip([*far, 0], [*first, *rest]))
    vz = {dz: hop(vb[dz], dz * I) for dz in far}

    def take_cv(index, after):
        group = groups[index]

        def kernel(me_ref, dens, *refs):
            outs, (buf, edge, edge2, sem) = refs[:g], refs[g:]
            offs = [dz * I + p for p in group for dz in order]
            for i, c in enumerate(gather(s, me_ref[0], dens, offs, None, buf, sem)):
                c.wait()
                pack(s, reader(s, buf, i, 0, edge), outs[i // O], i % O, 0)
                pack(s, reader(s, buf, i, n, edge2), outs[i // O], i % O, s.rows)

        k = O * g
        return call(
            kernel,
            [sds(O, 2 * s.rows, LANES)] * g,
            (me_arr, densities),
            [SM, HBM],
            [
                pltpu.VMEM((k, 2 * n, s.ng), BF16),
                pltpu.VMEM((k, n, LANES), BF16),
                pltpu.VMEM((k, n, LANES), BF16),
                pltpu.SemaphoreType.DMA((k,)),
            ],
            moved=8 * k * block,
            after=after,
        )

    def regroup(picks, count, parts, ins, after=()):
        def kernel(*refs):
            src, outs = refs[: len(ins)], refs[len(ins) :]
            for o, chosen in zip(outs, picks):
                for i, (a, b) in enumerate(chosen):
                    o[i] = src[a][b]

        return call(
            kernel,
            [sds(count, parts * s.rows, LANES)] * len(picks),
            ins,
            [VM] * len(ins),
            moved=4 * len(picks) * count * parts * block,
            after=after,
        )

    sent0 = take_cv(0, (rest[0],))
    near0 = [hop(x, p) for x, p in zip(sent0, groups[0])]
    sent1 = take_cv(1, (sent0[0],))
    near1 = [hop(x, p) for x, p in zip(sent1, groups[1])]

    def take_c(me_ref, dens, *refs):
        outs, sems = refs[:2], refs[2]
        copies = []
        for t, ps in enumerate(backs):
            copies += gather(s, me_ref[0], dens, [dz * I + p for dz in order for p in ps], 0, outs[t], sems.at[t])
        for c in copies:
            c.wait()

    own_c = call(
        take_c,
        [sds(O * len(ps), n, s.ng) for ps in backs],
        (me_arr, densities),
        [SM, HBM],
        [pltpu.SemaphoreType.DMA((2, O * h // 2))],
        moved=4 * O * h * block,
        after=(sent1[0],),
    )

    def onward(near, after):
        parts = regroup([[(j, zi) for j in range(g)] for zi in range(O)], g, 2, near, after)
        return [parts[0]] + [hop(x, dz * I) for dz, x in zip(far, parts[1:])]

    arrived = [onward(near0, (own_c[0],))]

    zs = [vb[0]] + [vz[dz] for dz in far]
    pieces = regroup([[(zi, j) for zi in range(O)] for j in range(h)], O, 1, zs, (arrived[0][0],))
    arrived.append(onward(near1, (pieces[0],)))
    vin = [pieces[0]] + [hop(x, p) for x, p in zip(pieces[1:], back[1:])]

    def screen_back(*refs):
        src, w_ref, outs, (v, sc) = refs[:h], refs[h], refs[h + 1 : 2 * h + 1], refs[2 * h + 1 :]
        for j in range(h):
            for a in range(O):
                unpack(s, src[j], a, 0, v, n * (j * O + a))
        screen(s, v, w_ref, sc)
        for j in range(h):
            for a in range(O):
                row = n * (j * O + a)
                pack(s, lambda lo, hi, row=row: sc[row : row + n, lo:hi], outs[j], a, 0)

    m_rows = n * h * O
    sb = call(
        screen_back,
        [sds(O, s.rows, LANES)] * h,
        (*vin, weights),
        [VM] * (h + 1),
        [pltpu.VMEM((m_rows, s.ng), BF16), pltpu.VMEM((m_rows, s.wide), BF16)],
        flops=2 * m_rows * s.ng * s.ng,
        moved=2 * s.ng * s.ng,
        after=(arrived[1][0],),
    )
    sin = [sb[0]] + [hop(x, p) for x, p in zip(sb[1:], back[1:])]
    half = len(backs[0])
    out0 = regroup([[(j, zi) for j in range(half)] for zi in range(O)], half, 1, sin[:half])
    sz0 = [out0[0]] + [hop(x, dz * I) for dz, x in zip(far, out0[1:])]

    def blocks_at_owner(index, after):
        count = O * g

        def kernel(*refs):
            src, w_ref, outs, (c, v, sc) = refs[:O], refs[O], refs[O + 1 : O + 1 + g], refs[O + 1 + g :]
            for zi in range(O):
                for j in range(g):
                    unpack(s, src[zi], j, 0, c, n * (zi * g + j))
                    unpack(s, src[zi], j, s.rows, v, n * (zi * g + j))
            screen(s, v, w_ref, sc)
            x = spread(s, c[...], sc[:, : s.ng])
            for j in range(g):
                total = 0.0
                for t in range(T):
                    sums = pick(
                        (O * T, count * n),
                        lambda r, k, j=j, t=t: (k // n == r // T * g + j) & (r % T == t),
                    )
                    total = total + jnp.dot(
                        sums, x[:, LANES * t : LANES * (t + 1)], preferred_element_type=F32
                    )
                outs[j][...] = total

        return call(
            kernel,
            [jax.ShapeDtypeStruct((O * T, LANES), F32)] * g,
            (*arrived[index], weights),
            [VM] * (O + 1),
            [
                pltpu.VMEM((n * count, s.ng), BF16),
                pltpu.VMEM((n * count, s.ng), BF16),
                pltpu.VMEM((n * count, s.wide), BF16),
            ],
            flops=2 * n * count * s.ng * s.ng,
            moved=2 * s.ng * s.ng,
            after=after,
        )

    done0 = blocks_at_owner(0, (out0[0],))
    done1 = blocks_at_owner(1, (done0[0],))
    returned = [hop(x, p) for x, p in zip([*done0, *done1], there)]

    rows2 = len(backs[1]) * s.rows
    extra = len(there) * T

    def outward1(*refs):
        src, small, outs = refs[: h - half], refs[h - half : h - half + 2 * g], refs[h - half + 2 * g :]
        blocks = jnp.concatenate([x[...] for x in small], axis=0).astype(BF16)
        turn = pick(
            (O * extra, O * extra),
            lambda r, k: (r % T == k % T) & (r // extra == k % (O * T) // T) & (r % extra // T == k // (O * T)),
        )
        turned = jnp.dot(turn, blocks, preferred_element_type=F32)
        for zi, o in enumerate(outs):
            for j in range(h - half):
                o[s.rows * j : s.rows * (j + 1), :] = src[j][zi]
            o[rows2 : rows2 + extra, :] = turned[extra * zi : extra * (zi + 1), :].astype(BF16)

    out1 = call(
        outward1,
        [sds(rows2 + extra, LANES)] * O,
        (*sin[half:], *returned),
        [VM] * (h - half + 2 * g),
        moved=4 * O * rows2 * LANES,
    )
    sz1 = [out1[0]] + [hop(x, dz * I) for dz, x in zip(far, out1[1:])]

    def finish0(me_ref, c_ref, *refs):
        src, (out, c, sc) = refs[:O], refs[O:]
        for zi in range(O):
            for j in range(half):
                row = n * (zi * half + j)
                c[row : row + n, :] = c_ref[zi * half + j]
                unpack(s, src[zi], j, 0, sc, row)
        out[...] = rows_of_pairs(s, me_ref[0], [dz * I + p for dz in order for p in backs[0]], c[...], sc[...])

    def finish1(me_ref, c_ref, *refs):
        src, (before, live_ref, out, c, sc) = refs[:O], refs[O:]
        me, k = me_ref[0], h - half
        for zi in range(O):
            for j in range(k):
                row = n * (zi * k + j)
                c[row : row + n, :] = c_ref[zi * k + j]
                unpack(s, src[zi], None, s.rows * j, sc, row)
        r = rows_of_pairs(s, me, [dz * I + p for dz in order for p in backs[1]], c[...], sc[...])
        small = jnp.concatenate([x[rows2 : rows2 + extra, :].astype(F32) for x in src], axis=0).astype(BF16)
        offs = [dz * I + p for dz in order for p in there]
        placed = [
            jnp.dot(
                pick((N, O * extra), lambda q, x, t=t: (q == (table(x // T, offs) ^ me)) & (x % T == t)),
                small,
                preferred_element_type=F32,
            )
            for t in range(T)
        ]
        r = r + before[...] + jnp.concatenate(placed, axis=1)
        out[...] = (r * live_ref[...].astype(F32)).astype(BF16)

    def scratch(ps):
        return [pltpu.VMEM((n * O * len(ps), s.ng), BF16)] * 2

    partial = call(
        finish0,
        [jax.ShapeDtypeStruct((N, n * n), F32)],
        (me_arr, own_c[0], *sz0),
        [SM] + [VM] * (1 + O),
        scratch(backs[0]),
        flops=2 * m_rows * s.ng * n,
        moved=4 * m_rows * s.ng,
        after=(out1[0],),
    )[0]
    return call(
        finish1,
        [sds(N, n * n)],
        (me_arr, own_c[1], *sz1, partial, live),
        [SM] + [VM] * (3 + O),
        scratch(backs[1]),
        flops=2 * m_rows * s.ng * n,
        moved=4 * m_rows * s.ng,
    )[0][:, None, :]


def plain(densities, screening, live):
    pairs = densities.shape[2] // 2
    arrived = lax.all_to_all(densities, "pb", split_axis=0, concat_axis=0, tiled=True)
    screened = jnp.einsum(
        "nkbh,gh->nkbg", arrived[:, :, pairs:, :], screening[0], preferred_element_type=F32
    ).astype(BF16)
    blocks = jnp.einsum("nkag,nkbg->nkab", arrived[:, :, :pairs, :], screened, preferred_element_type=F32)
    blocks = blocks.reshape(blocks.shape[0], blocks.shape[1], -1).astype(BF16)
    result = lax.all_to_all(blocks, "pb", split_axis=0, concat_axis=0, tiled=True)
    return result * live.astype(BF16)[:, :, None]


def solution(mesh):
    devices = mesh.shape["pb"]

    def on_device(densities, screening, live):
        s = Sizes(densities.shape, devices)
        if s.q == devices and s.fits():
            return fast(s, densities, screening, live)
        return plain(densities, screening, live)

    in_specs = (P(None, "pb", None, None), P("pb", None, None), P(None, "pb"))
    return jax.shard_map(
        on_device, mesh=mesh, in_specs=in_specs, out_specs=P(None, "pb", None), check_vma=False
    )
```

```python
import jax
import jax.numpy as jnp
from jax import lax
from jax.experimental import pallas as pl
from jax.experimental.pallas import tpu as pltpu
from jax.sharding import PartitionSpec as P


BF16, F32 = jnp.bfloat16, jnp.float32
LANES = 128
HALF = LANES // 2
COLS = 256


VM = pl.BlockSpec(memory_space=pltpu.VMEM)
SM = pl.BlockSpec(memory_space=pltpu.SMEM)
ANY = pl.BlockSpec(memory_space=pl.ANY)
HBM = pl.BlockSpec(memory_space=pltpu.HBM)


def split(devices):
    outer = 2 ** ((devices.bit_length() - 1) // 2)
    return outer, devices // outer


class Sizes:
    def __init__(self, shape, devices):
        self.q, _, both, self.ng = shape
        self.pairs = both // 2
        self.full, self.tail = divmod(self.ng, LANES)
        self.rows = self.pairs * self.full + (self.pairs // 2 if self.tail else 0)
        self.wide = LANES * (self.full + (1 if self.tail else 0))
        self.devices = devices
        self.outer, self.inner = split(devices)

    def fits(self):
        power = self.devices & (self.devices - 1) == 0
        return power and self.inner >= 4 and self.pairs == 16 and 0 < self.tail <= HALF


def call(kernel, outs, ins, specs, scratch=(), flops=0, moved=0, after=()):
    k, a = len(ins), len(after)

    def body(*refs):
        kernel(*refs[:k], *refs[k + a :])

    return pallas(body, outs, specs, a, scratch, flops, moved)(*ins, *after)


def pallas(body, outs, specs, a, scratch, flops, moved):
    return pl.pallas_call(
        body,
        out_shape=tuple(outs),
        in_specs=[*specs, *[ANY] * a],
        out_specs=tuple(pl.BlockSpec(memory_space=pltpu.VMEM) for _ in outs),
        scratch_shapes=list(scratch),
        compiler_params=pltpu.CompilerParams(vmem_limit_bytes=24 << 20),
        cost_estimate=pl.CostEstimate(flops=flops, bytes_accessed=moved, transcendentals=0),
    )


def pack(s, read, dst, b, base):
    n = s.pairs
    for j in range(s.full):
        dst[b, base + n * j : base + n * (j + 1), :] = read(LANES * j, LANES * (j + 1))
    last = read(LANES * s.full, s.wide).astype(F32)
    lane = lax.broadcasted_iota(jnp.int32, (n // 2, LANES), 1)
    folded = jnp.where(lane < HALF, last[: n // 2], pltpu.roll(last[n // 2 :], HALF, 1))
    dst[b, base + n * s.full : base + s.rows, :] = folded.astype(BF16)


def unpack(s, src, b, base, dst, row):
    n = s.pairs
    src = src if b is None else src.at[b]
    for j in range(s.full):
        dst[row : row + n, LANES * j : LANES * (j + 1)] = src[base + n * j : base + n * (j + 1), :]
    folded = src[base + n * s.full : base + s.rows, :].astype(F32)
    last = jnp.concatenate([folded, pltpu.roll(folded, HALF, 1)], axis=0).astype(BF16)
    dst[row : row + n, LANES * s.full : s.ng] = last[:, : s.tail]


def nt(x, y):
    return lax.dot_general(x, y, (((1,), (1,)), ((), ())), preferred_element_type=F32)


def screen(s, v, w_ref, out):
    for lo in range(0, s.ng, COLS):
        hi = min(lo + COLS, s.ng)
        out[:, lo:hi] = nt(v[...], w_ref[0, lo:hi, :]).astype(BF16)


def spread(s, c, sc):
    n, count = s.pairs, c.shape[0]
    full = nt(c, sc)
    r = lax.broadcasted_iota(jnp.int32, (count, count), 0)
    k = lax.broadcasted_iota(jnp.int32, (count, count), 1)
    own = jnp.where(r // n == k // n, full, 0.0).astype(BF16)
    e = lax.broadcasted_iota(jnp.int32, (count, n * n), 0)
    f = lax.broadcasted_iota(jnp.int32, (count, n * n), 1)
    copies = jnp.where(e % n == f % n, 1.0, 0.0).astype(BF16)
    x = jnp.dot(own, copies, preferred_element_type=F32)
    return jnp.where(f // n == e % n, x, 0.0).astype(BF16)


def pick(shape, wanted):
    row = lax.broadcasted_iota(jnp.int32, shape, 0)
    column = lax.broadcasted_iota(jnp.int32, shape, 1)
    return jnp.where(wanted(row, column), 1.0, 0.0).astype(BF16)


def table(index, values):
    out = jnp.zeros_like(index)
    for i, value in enumerate(values):
        out = jnp.where(index == i, value, out)
    return out


def rows_of_pairs(s, me, offsets, c, sc):
    x = spread(s, c, sc)
    place = pick((s.devices, x.shape[0]), lambda q, r: q == (table(r // s.pairs, offsets) ^ me))
    return jnp.dot(place, x, preferred_element_type=F32)


def gather(s, me, dens, offsets, half, buf, sem):
    lo, n = (0, 2 * s.pairs) if half is None else (half * s.pairs, s.pairs)
    copies = [
        pltpu.make_async_copy(dens.at[me ^ m, 0, pl.ds(lo, n), :], buf.at[i], sem.at[i])
        for i, m in enumerate(offsets)
    ]
    for c in copies:
        c.start()
    return copies


def reader(s, buf, i, row, edge):
    def read(lo, hi):
        if hi <= s.ng:
            return buf[i, row : row + s.pairs, lo:hi]
        edge[i, :, : s.tail] = buf[i, row : row + s.pairs, lo : s.ng]
        return edge[i]

    return read


def parts_of(devices):
    outer, count = split(devices)
    inner = sorted(range(count), key=lambda p: (bin(p).count("1"), p))
    back, there = inner[: count // 2], inner[count // 2 :]
    half, most = len(there) // 2, len(back) * 3 // 4
    return [back[:most], back[most:]], [there[:half], there[half:]], list(range(outer - 1, 0, -1))


def fast(s, densities, weights, live):
    me_arr = lax.axis_index("pb").astype(jnp.int32).reshape(1)
    O, I, N, n = s.outer, s.inner, s.devices, s.pairs
    backs, (later, sooner), far = parts_of(N)
    order = [0, *far]
    back, there = backs[0] + backs[1], later + sooner
    h, g = len(back), len(later)
    T = n * n // LANES
    block = n * s.ng

    def sds(*shape):
        return jax.ShapeDtypeStruct(shape, BF16)

    def hop(x, m):
        return lax.ppermute(x, "pb", [(d, d ^ m) for d in range(N)])

    densities = pltpu.with_memory_space_constraint(densities, pltpu.HBM)

    def take_v(zs, after):
        def kernel(me_ref, dens, *refs):
            outs, (buf, edge, sem) = refs[: len(zs)], refs[len(zs) :]
            offs = [dz * I + p for dz in zs for p in back]
            for i, c in enumerate(gather(s, me_ref[0], dens, offs, 1, buf, sem)):
                c.wait()
                pack(s, reader(s, buf, i, 0, edge), outs[i // h], i % h, 0)

        k = len(zs) * h
        return call(
            kernel,
            [sds(h, s.rows, LANES)] * len(zs),
            (me_arr, densities),
            [SM, HBM],
            [pltpu.VMEM((k, n, s.ng), BF16), pltpu.VMEM((k, n, LANES), BF16), pltpu.SemaphoreType.DMA((k,))],
            moved=4 * k * block,
            after=after,
        )

    first = take_v(far[:1], ())
    rest = take_v([*far[1:], 0], (first[0],))
    vb = dict(zip([*far, 0], [*first, *rest]))
    vz = {dz: hop(vb[dz], dz * I) for dz in far}

    def take_cv(picks, count, after):
        def kernel(me_ref, dens, *refs):
            outs, (buf, edge, edge2, sem) = refs[: len(picks)], refs[len(picks) :]
            offs = [m for chosen in picks for m in chosen]
            for i, c in enumerate(gather(s, me_ref[0], dens, offs, None, buf, sem)):
                c.wait()
                pack(s, reader(s, buf, i, 0, edge), outs[i // count], i % count, 0)
                pack(s, reader(s, buf, i, n, edge2), outs[i // count], i % count, s.rows)

        k = len(picks) * count
        return call(
            kernel,
            [sds(count, 2 * s.rows, LANES)] * len(picks),
            (me_arr, densities),
            [SM, HBM],
            [
                pltpu.VMEM((k, 2 * n, s.ng), BF16),
                pltpu.VMEM((k, n, LANES), BF16),
                pltpu.VMEM((k, n, LANES), BF16),
                pltpu.SemaphoreType.DMA((k,)),
            ],
            moved=8 * k * block,
            after=after,
        )

    def regroup(picks, count, parts, ins, after=()):
        def kernel(*refs):
            src, outs = refs[: len(ins)], refs[len(ins) :]
            for o, chosen in zip(outs, picks):
                for i, (a, b) in enumerate(chosen):
                    o[i] = src[a][b]

        return call(
            kernel,
            [sds(count, parts * s.rows, LANES)] * len(picks),
            ins,
            [VM] * len(ins),
            moved=4 * len(picks) * count * parts * block,
            after=after,
        )

    sent = take_cv([[dz * I + p for dz in order] for p in sooner], O, (rest[0],))
    near = [hop(x, p) for x, p in zip(sent, sooner)]
    whole = take_cv([[dz * I + p for p in later] for dz in order], g, (sent[0],))
    azf = [whole[0]] + [hop(x, dz * I) for dz, x in zip(far, whole[1:])]

    def take_c(me_ref, dens, *refs):
        outs, sems = refs[:2], refs[2]
        copies = []
        for t, ps in enumerate(backs):
            copies += gather(s, me_ref[0], dens, [dz * I + p for dz in order for p in ps], 0, outs[t], sems.at[t])
        for c in copies:
            c.wait()

    own_c = call(
        take_c,
        [sds(O * len(ps), n, s.ng) for ps in backs],
        (me_arr, densities),
        [SM, HBM],
        [pltpu.SemaphoreType.DMA((2, O * h))],
        moved=4 * O * h * block,
        after=(whole[0],),
    )

    zs = [vb[0]] + [vz[dz] for dz in far]
    pieces = regroup([[(zi, j) for zi in range(O)] for j in range(h)], O, 1, zs, (own_c[0],))
    vin = [pieces[0]] + [hop(x, p) for x, p in zip(pieces[1:], back[1:])]

    parts = regroup([[(j, zi) for j in range(g)] for zi in range(O)], g, 2, near, (pieces[0],))
    azn = [parts[0]] + [hop(x, dz * I) for dz, x in zip(far, parts[1:])]

    def screen_back(*refs):
        src, w_ref, outs, (v, sc) = refs[:h], refs[h], refs[h + 1 : 2 * h + 1], refs[2 * h + 1 :]
        for j in range(h):
            for a in range(O):
                unpack(s, src[j], a, 0, v, n * (j * O + a))
        screen(s, v, w_ref, sc)
        for j in range(h):
            for a in range(O):
                row = n * (j * O + a)
                pack(s, lambda lo, hi, row=row: sc[row : row + n, lo:hi], outs[j], a, 0)

    m_rows = n * h * O
    sb = call(
        screen_back,
        [sds(O, s.rows, LANES)] * h,
        (*vin, weights),
        [VM] * (h + 1),
        [pltpu.VMEM((m_rows, s.ng), BF16), pltpu.VMEM((m_rows, s.wide), BF16)],
        flops=2 * m_rows * s.ng * s.ng,
        moved=2 * s.ng * s.ng,
        after=(parts[0],),
    )
    sin = [sb[0]] + [hop(x, p) for x, p in zip(sb[1:], back[1:])]
    half = len(backs[0])
    mine = regroup([[(zi, j) for zi in range(O)] for j in range(g)], O, 2, azf, (sb[0],))
    fin = [hop(x, p) for x, p in zip(mine, later)]
    out0 = regroup([[(j, zi) for j in range(half)] for zi in range(O)], half, 1, sin[:half], (mine[0],))
    sz0 = [out0[0]] + [hop(x, dz * I) for dz, x in zip(far, out0[1:])]

    def blocks_at_owner(arrived, by_outer, after):
        count, k = O * g, len(arrived)

        def kernel(*refs):
            src, w_ref, outs, (c, v, sc) = refs[:k], refs[k], refs[k + 1 : k + 1 + g], refs[k + 1 + g :]
            for zi in range(O):
                for j in range(g):
                    a, b = (zi, j) if by_outer else (j, zi)
                    unpack(s, src[a], b, 0, c, n * (zi * g + j))
                    unpack(s, src[a], b, s.rows, v, n * (zi * g + j))
            screen(s, v, w_ref, sc)
            x = spread(s, c[...], sc[:, : s.ng])
            for j in range(g):
                total = 0.0
                for t in range(T):
                    sums = pick(
                        (O * T, count * n),
                        lambda r, k, j=j, t=t: (k // n == r // T * g + j) & (r % T == t),
                    )
                    total = total + jnp.dot(
                        sums, x[:, LANES * t : LANES * (t + 1)], preferred_element_type=F32
                    )
                outs[j][...] = total

        return call(
            kernel,
            [jax.ShapeDtypeStruct((O * T, LANES), F32)] * g,
            (*arrived, weights),
            [VM] * (k + 1),
            [
                pltpu.VMEM((n * count, s.ng), BF16),
                pltpu.VMEM((n * count, s.ng), BF16),
                pltpu.VMEM((n * count, s.wide), BF16),
            ],
            flops=2 * n * count * s.ng * s.ng,
            moved=2 * s.ng * s.ng,
            after=after,
        )

    done0 = blocks_at_owner(fin, False, (out0[0],))
    done1 = blocks_at_owner(azn, True, (done0[0],))
    returned = [hop(x, p) for x, p in zip([*done0, *done1], there)]

    rows2 = len(backs[1]) * s.rows
    extra = len(there) * T

    def outward1(*refs):
        src, small, outs = refs[: h - half], refs[h - half : h - half + 2 * g], refs[h - half + 2 * g :]
        blocks = jnp.concatenate([x[...] for x in small], axis=0).astype(BF16)
        turn = pick(
            (O * extra, O * extra),
            lambda r, k: (r % T == k % T) & (r // extra == k % (O * T) // T) & (r % extra // T == k // (O * T)),
        )
        turned = jnp.dot(turn, blocks, preferred_element_type=F32)
        for zi, o in enumerate(outs):
            for j in range(h - half):
                o[s.rows * j : s.rows * (j + 1), :] = src[j][zi]
            o[rows2 : rows2 + extra, :] = turned[extra * zi : extra * (zi + 1), :].astype(BF16)

    out1 = call(
        outward1,
        [sds(rows2 + extra, LANES)] * O,
        (*sin[half:], *returned),
        [VM] * (h - half + 2 * g),
        moved=4 * O * rows2 * LANES,
    )
    sz1 = [out1[0]] + [hop(x, dz * I) for dz, x in zip(far, out1[1:])]

    def finish0(me_ref, c_ref, *refs):
        src, (out, c, sc) = refs[:O], refs[O:]
        for zi in range(O):
            for j in range(half):
                row = n * (zi * half + j)
                c[row : row + n, :] = c_ref[zi * half + j]
                unpack(s, src[zi], j, 0, sc, row)
        out[...] = rows_of_pairs(s, me_ref[0], [dz * I + p for dz in order for p in backs[0]], c[...], sc[...])

    def finish1(me_ref, c_ref, *refs):
        src, (before, live_ref, out, c, sc) = refs[:O], refs[O:]
        me, k = me_ref[0], h - half
        for zi in range(O):
            for j in range(k):
                row = n * (zi * k + j)
                c[row : row + n, :] = c_ref[zi * k + j]
                unpack(s, src[zi], None, s.rows * j, sc, row)
        r = rows_of_pairs(s, me, [dz * I + p for dz in order for p in backs[1]], c[...], sc[...])
        small = jnp.concatenate([x[rows2 : rows2 + extra, :].astype(F32) for x in src], axis=0).astype(BF16)
        offs = [dz * I + p for dz in order for p in there]
        placed = [
            jnp.dot(
                pick((N, O * extra), lambda q, x, t=t: (q == (table(x // T, offs) ^ me)) & (x % T == t)),
                small,
                preferred_element_type=F32,
            )
            for t in range(T)
        ]
        r = r + before[...] + jnp.concatenate(placed, axis=1)
        out[...] = (r * live_ref[...].astype(F32)).astype(BF16)

    def scratch(ps):
        return [pltpu.VMEM((n * O * len(ps), s.ng), BF16)] * 2

    partial = call(
        finish0,
        [jax.ShapeDtypeStruct((N, n * n), F32)],
        (me_arr, own_c[0], *sz0),
        [SM] + [VM] * (1 + O),
        scratch(backs[0]),
        flops=2 * m_rows * s.ng * n,
        moved=4 * m_rows * s.ng,
        after=(out1[0],),
    )[0]
    return call(
        finish1,
        [sds(N, n * n)],
        (me_arr, own_c[1], *sz1, partial, live),
        [SM] + [VM] * (3 + O),
        scratch(backs[1]),
        flops=2 * m_rows * s.ng * n,
        moved=4 * m_rows * s.ng,
    )[0][:, None, :]


def plain(densities, screening, live):
    pairs = densities.shape[2] // 2
    arrived = lax.all_to_all(densities, "pb", split_axis=0, concat_axis=0, tiled=True)
    screened = jnp.einsum(
        "nkbh,gh->nkbg", arrived[:, :, pairs:, :], screening[0], preferred_element_type=F32
    ).astype(BF16)
    blocks = jnp.einsum("nkag,nkbg->nkab", arrived[:, :, :pairs, :], screened, preferred_element_type=F32)
    blocks = blocks.reshape(blocks.shape[0], blocks.shape[1], -1).astype(BF16)
    result = lax.all_to_all(blocks, "pb", split_axis=0, concat_axis=0, tiled=True)
    return result * live.astype(BF16)[:, :, None]


def solution(mesh):
    devices = mesh.shape["pb"]

    def on_device(densities, screening, live):
        s = Sizes(densities.shape, devices)
        if s.q == devices and s.fits():
            return fast(s, densities, screening, live)
        return plain(densities, screening, live)

    in_specs = (P(None, "pb", None, None), P("pb", None, None), P(None, "pb"))
    return jax.shard_map(
        on_device, mesh=mesh, in_specs=in_specs, out_specs=P(None, "pb", None), check_vma=False
    )
```

```python
import jax
import jax.numpy as jnp
from jax import lax
from jax.experimental import pallas as pl
from jax.experimental.pallas import tpu as pltpu
from jax.sharding import PartitionSpec as P


BF16, F32 = jnp.bfloat16, jnp.float32
LANES = 128
HALF = LANES // 2
COLS = 256


VM = pl.BlockSpec(memory_space=pltpu.VMEM)
SM = pl.BlockSpec(memory_space=pltpu.SMEM)
ANY = pl.BlockSpec(memory_space=pl.ANY)
HBM = pl.BlockSpec(memory_space=pltpu.HBM)


def split(devices):
    outer = 2 ** ((devices.bit_length() - 1) // 2)
    return outer, devices // outer


class Sizes:
    def __init__(self, shape, devices):
        self.q, _, both, self.ng = shape
        self.pairs = both // 2
        self.full, self.tail = divmod(self.ng, LANES)
        self.rows = self.pairs * self.full + (self.pairs // 2 if self.tail else 0)
        self.wide = LANES * (self.full + (1 if self.tail else 0))
        self.devices = devices
        self.outer, self.inner = split(devices)

    def fits(self):
        power = self.devices & (self.devices - 1) == 0
        return power and self.inner >= 4 and self.pairs == 16 and 0 < self.tail <= HALF


def call(kernel, outs, ins, specs, scratch=(), flops=0, moved=0, after=()):
    k, a = len(ins), len(after)

    def body(*refs):
        kernel(*refs[:k], *refs[k + a :])

    return pallas(body, outs, specs, a, scratch, flops, moved)(*ins, *after)


def pallas(body, outs, specs, a, scratch, flops, moved):
    return pl.pallas_call(
        body,
        out_shape=tuple(outs),
        in_specs=[*specs, *[ANY] * a],
        out_specs=tuple(pl.BlockSpec(memory_space=pltpu.VMEM) for _ in outs),
        scratch_shapes=list(scratch),
        compiler_params=pltpu.CompilerParams(vmem_limit_bytes=24 << 20),
        cost_estimate=pl.CostEstimate(flops=flops, bytes_accessed=moved, transcendentals=0),
    )


def pack(s, read, dst, b, base):
    n = s.pairs
    for j in range(s.full):
        dst[b, base + n * j : base + n * (j + 1), :] = read(LANES * j, LANES * (j + 1))
    last = read(LANES * s.full, s.wide).astype(F32)
    lane = lax.broadcasted_iota(jnp.int32, (n // 2, LANES), 1)
    folded = jnp.where(lane < HALF, last[: n // 2], pltpu.roll(last[n // 2 :], HALF, 1))
    dst[b, base + n * s.full : base + s.rows, :] = folded.astype(BF16)


def unpack(s, src, b, base, dst, row):
    n = s.pairs
    src = src if b is None else src.at[b]
    for j in range(s.full):
        dst[row : row + n, LANES * j : LANES * (j + 1)] = src[base + n * j : base + n * (j + 1), :]
    folded = src[base + n * s.full : base + s.rows, :].astype(F32)
    last = jnp.concatenate([folded, pltpu.roll(folded, HALF, 1)], axis=0).astype(BF16)
    dst[row : row + n, LANES * s.full : s.ng] = last[:, : s.tail]


def nt(x, y):
    return lax.dot_general(x, y, (((1,), (1,)), ((), ())), preferred_element_type=F32)


def screen(s, v, w_ref, out):
    for lo in range(0, s.ng, COLS):
        hi = min(lo + COLS, s.ng)
        out[:, lo:hi] = nt(v[...], w_ref[0, lo:hi, :]).astype(BF16)


def spread(s, c, sc):
    n, count = s.pairs, c.shape[0]
    full = nt(c, sc)
    r = lax.broadcasted_iota(jnp.int32, (count, count), 0)
    k = lax.broadcasted_iota(jnp.int32, (count, count), 1)
    own = jnp.where(r // n == k // n, full, 0.0).astype(BF16)
    e = lax.broadcasted_iota(jnp.int32, (count, n * n), 0)
    f = lax.broadcasted_iota(jnp.int32, (count, n * n), 1)
    copies = jnp.where(e % n == f % n, 1.0, 0.0).astype(BF16)
    x = jnp.dot(own, copies, preferred_element_type=F32)
    return jnp.where(f // n == e % n, x, 0.0).astype(BF16)


def pick(shape, wanted):
    row = lax.broadcasted_iota(jnp.int32, shape, 0)
    column = lax.broadcasted_iota(jnp.int32, shape, 1)
    return jnp.where(wanted(row, column), 1.0, 0.0).astype(BF16)


def table(index, values):
    out = jnp.zeros_like(index)
    for i, value in enumerate(values):
        out = jnp.where(index == i, value, out)
    return out


def rows_of_pairs(s, me, offsets, c, sc):
    x = spread(s, c, sc)
    place = pick((s.devices, x.shape[0]), lambda q, r: q == (table(r // s.pairs, offsets) ^ me))
    return jnp.dot(place, x, preferred_element_type=F32)


def gather(s, me, dens, offsets, half, buf, sem):
    lo, n = (0, 2 * s.pairs) if half is None else (half * s.pairs, s.pairs)
    copies = [
        pltpu.make_async_copy(dens.at[me ^ m, 0, pl.ds(lo, n), :], buf.at[i], sem.at[i])
        for i, m in enumerate(offsets)
    ]
    for c in copies:
        c.start()
    return copies


def reader(s, buf, i, row, edge):
    def read(lo, hi):
        if hi <= s.ng:
            return buf[i, row : row + s.pairs, lo:hi]
        edge[i, :, : s.tail] = buf[i, row : row + s.pairs, lo : s.ng]
        return edge[i]

    return read


def parts_of(devices):
    outer, count = split(devices)
    inner = sorted(range(count), key=lambda p: (bin(p).count("1"), p))
    back, there = inner[: count // 2], inner[count // 2 :]
    half = len(there) // 2
    return back, (there[:half], there[half:]), list(range(outer - 1, 0, -1))


def fast(s, densities, weights, live):
    me_arr = lax.axis_index("pb").astype(jnp.int32).reshape(1)
    O, I, N, n = s.outer, s.inner, s.devices, s.pairs
    back, (later, sooner), far = parts_of(N)
    order = [0, *far]
    there = later + sooner
    h, g = len(back), len(later)
    T = n * n // LANES
    block = n * s.ng

    def sds(*shape):
        return jax.ShapeDtypeStruct(shape, BF16)

    def hop(x, m):
        return lax.ppermute(x, "pb", [(d, d ^ m) for d in range(N)])

    densities = pltpu.with_memory_space_constraint(densities, pltpu.HBM)

    def take_v(zs, after):
        def kernel(me_ref, dens, *refs):
            outs, (buf, edge, sem) = refs[: len(zs)], refs[len(zs) :]
            offs = [dz * I + p for dz in zs for p in back]
            for i, c in enumerate(gather(s, me_ref[0], dens, offs, 1, buf, sem)):
                c.wait()
                pack(s, reader(s, buf, i, 0, edge), outs[i // h], i % h, 0)

        k = len(zs) * h
        return call(
            kernel,
            [sds(h, s.rows, LANES)] * len(zs),
            (me_arr, densities),
            [SM, HBM],
            [pltpu.VMEM((k, n, s.ng), BF16), pltpu.VMEM((k, n, LANES), BF16), pltpu.SemaphoreType.DMA((k,))],
            moved=4 * k * block,
            after=after,
        )

    first = take_v(far[:1], ())
    rest = take_v([*far[1:], 0], (first[0],))
    vb = dict(zip([*far, 0], [*first, *rest]))
    vz = {dz: hop(vb[dz], dz * I) for dz in far}

    def take_cv(picks, count, after):
        def kernel(me_ref, dens, *refs):
            outs, (buf, edge, edge2, sem) = refs[: len(picks)], refs[len(picks) :]
            offs = [m for chosen in picks for m in chosen]
            for i, c in enumerate(gather(s, me_ref[0], dens, offs, None, buf, sem)):
                c.wait()
                pack(s, reader(s, buf, i, 0, edge), outs[i // count], i % count, 0)
                pack(s, reader(s, buf, i, n, edge2), outs[i // count], i % count, s.rows)

        k = len(picks) * count
        return call(
            kernel,
            [sds(count, 2 * s.rows, LANES)] * len(picks),
            (me_arr, densities),
            [SM, HBM],
            [
                pltpu.VMEM((k, 2 * n, s.ng), BF16),
                pltpu.VMEM((k, n, LANES), BF16),
                pltpu.VMEM((k, n, LANES), BF16),
                pltpu.SemaphoreType.DMA((k,)),
            ],
            moved=8 * k * block,
            after=after,
        )

    def regroup(picks, count, parts, ins, after=()):
        def kernel(*refs):
            src, outs = refs[: len(ins)], refs[len(ins) :]
            for o, chosen in zip(outs, picks):
                for i, (a, b) in enumerate(chosen):
                    o[i] = src[a][b]

        return call(
            kernel,
            [sds(count, parts * s.rows, LANES)] * len(picks),
            ins,
            [VM] * len(ins),
            moved=4 * len(picks) * count * parts * block,
            after=after,
        )

    sent = take_cv([[dz * I + p for dz in order] for p in sooner], O, (rest[0],))
    near = [hop(x, p) for x, p in zip(sent, sooner)]
    whole = take_cv([[dz * I + p for p in later] for dz in order], g, (sent[0],))
    azf = [whole[0]] + [hop(x, dz * I) for dz, x in zip(far, whole[1:])]

    def take_c(me_ref, dens, out, sem):
        for c in gather(s, me_ref[0], dens, [dz * I + p for dz in order for p in back], 0, out, sem):
            c.wait()

    own_c = call(
        take_c,
        [sds(O * h, n, s.ng)],
        (me_arr, densities),
        [SM, HBM],
        [pltpu.SemaphoreType.DMA((O * h,))],
        moved=4 * O * h * block,
        after=(whole[0],),
    )

    zs = [vb[0]] + [vz[dz] for dz in far]
    pieces = regroup([[(zi, j) for zi in range(O)] for j in range(h)], O, 1, zs, (own_c[0],))
    vin = [pieces[0]] + [hop(x, p) for x, p in zip(pieces[1:], back[1:])]

    parts = regroup([[(j, zi) for j in range(g)] for zi in range(O)], g, 2, near, (pieces[0],))
    azn = [parts[0]] + [hop(x, dz * I) for dz, x in zip(far, parts[1:])]

    def screen_back(*refs):
        src, w_ref, outs, (v, sc) = refs[:h], refs[h], refs[h + 1 : 2 * h + 1], refs[2 * h + 1 :]
        for j in range(h):
            for a in range(O):
                unpack(s, src[j], a, 0, v, n * (j * O + a))
        screen(s, v, w_ref, sc)
        for j in range(h):
            for a in range(O):
                row = n * (j * O + a)
                pack(s, lambda lo, hi, row=row: sc[row : row + n, lo:hi], outs[j], a, 0)

    m_rows = n * h * O
    sb = call(
        screen_back,
        [sds(O, s.rows, LANES)] * h,
        (*vin, weights),
        [VM] * (h + 1),
        [pltpu.VMEM((m_rows, s.ng), BF16), pltpu.VMEM((m_rows, s.wide), BF16)],
        flops=2 * m_rows * s.ng * s.ng,
        moved=2 * s.ng * s.ng,
        after=(parts[0],),
    )
    sin = [sb[0]] + [hop(x, p) for x, p in zip(sb[1:], back[1:])]
    mine = regroup([[(zi, j) for zi in range(O)] for j in range(g)], O, 2, azf, (sb[0],))
    fin = [hop(x, p) for x, p in zip(mine, later)]
    back_z = regroup([[(j, zi) for j in range(h)] for zi in range(O)], h, 1, sin, (mine[0],))
    sz = [back_z[0]] + [hop(x, dz * I) for dz, x in zip(far, back_z[1:])]

    def blocks_at_owner(arrived, by_outer, after):
        count, k = O * g, len(arrived)

        def kernel(*refs):
            src, w_ref, outs, (c, v, sc) = refs[:k], refs[k], refs[k + 1 : k + 1 + g], refs[k + 1 + g :]
            for zi in range(O):
                for j in range(g):
                    a, b = (zi, j) if by_outer else (j, zi)
                    unpack(s, src[a], b, 0, c, n * (zi * g + j))
                    unpack(s, src[a], b, s.rows, v, n * (zi * g + j))
            screen(s, v, w_ref, sc)
            x = spread(s, c[...], sc[:, : s.ng])
            for j in range(g):
                total = 0.0
                for t in range(T):
                    sums = pick(
                        (O * T, count * n),
                        lambda r, k, j=j, t=t: (k // n == r // T * g + j) & (r % T == t),
                    )
                    total = total + jnp.dot(
                        sums, x[:, LANES * t : LANES * (t + 1)], preferred_element_type=F32
                    )
                outs[j][...] = total

        return call(
            kernel,
            [jax.ShapeDtypeStruct((O * T, LANES), F32)] * g,
            (*arrived, weights),
            [VM] * (k + 1),
            [
                pltpu.VMEM((n * count, s.ng), BF16),
                pltpu.VMEM((n * count, s.ng), BF16),
                pltpu.VMEM((n * count, s.wide), BF16),
            ],
            flops=2 * n * count * s.ng * s.ng,
            moved=2 * s.ng * s.ng,
            after=after,
        )

    done1 = blocks_at_owner(azn, True, (back_z[0],))
    done0 = blocks_at_owner(fin, False, (done1[0],))
    returned = [hop(x, p) for x, p in zip([*done0, *done1], there)]

    extra = len(there) * T

    def turn(*refs):
        small, outs = refs[: 2 * g], refs[2 * g :]
        blocks = jnp.concatenate([x[...] for x in small], axis=0).astype(BF16)
        order01 = pick(
            (O * extra, O * extra),
            lambda r, k: (r % T == k % T) & (r // extra == k % (O * T) // T) & (r % extra // T == k // (O * T)),
        )
        turned = jnp.dot(order01, blocks, preferred_element_type=F32)
        for zi, o in enumerate(outs):
            o[...] = turned[extra * zi : extra * (zi + 1), :]

    small = call(
        turn, [jax.ShapeDtypeStruct((extra, LANES), F32)] * O, returned, [VM] * (2 * g), moved=8 * O * extra * LANES
    )
    kz = [small[0]] + [hop(x, dz * I) for dz, x in zip(far, small[1:])]

    def finish0(me_ref, c_ref, *refs):
        src, (out, c, sc) = refs[:O], refs[O:]
        for zi in range(O):
            for j in range(h):
                row = n * (zi * h + j)
                c[row : row + n, :] = c_ref[zi * h + j]
                unpack(s, src[zi], j, 0, sc, row)
        r, half = 0.0, m_rows // 2
        offs = [dz * I + p for dz in order for p in back]
        for i, lo in enumerate((0, half)):
            chosen = offs[i * len(offs) // 2 : (i + 1) * len(offs) // 2]
            r = r + rows_of_pairs(s, me_ref[0], chosen, c[lo : lo + half, :], sc[lo : lo + half, :])
        out[...] = r

    def finish1(me_ref, *refs):
        src, (before, live_ref, out) = refs[:O], refs[O:]
        rows = jnp.concatenate([x[...] for x in src], axis=0).astype(BF16)
        offs = [dz * I + p for dz in order for p in there]
        placed = [
            jnp.dot(
                pick((N, O * extra), lambda q, x, t=t: (q == (table(x // T, offs) ^ me_ref[0])) & (x % T == t)),
                rows,
                preferred_element_type=F32,
            )
            for t in range(T)
        ]
        r = before[...] + jnp.concatenate(placed, axis=1)
        out[...] = (r * live_ref[...].astype(F32)).astype(BF16)

    partial = call(
        finish0,
        [jax.ShapeDtypeStruct((N, n * n), F32)],
        (me_arr, own_c[0], *sz),
        [SM] + [VM] * (1 + O),
        [pltpu.VMEM((m_rows, s.ng), BF16)] * 2,
        flops=2 * m_rows * s.ng * n,
        moved=4 * m_rows * s.ng,
        after=(small[0],),
    )[0]
    return call(
        finish1, [sds(N, n * n)], (me_arr, *kz, partial, live), [SM] + [VM] * (2 + O), moved=8 * N * n * n
    )[0][:, None, :]


def plain(densities, screening, live):
    pairs = densities.shape[2] // 2
    arrived = lax.all_to_all(densities, "pb", split_axis=0, concat_axis=0, tiled=True)
    screened = jnp.einsum(
        "nkbh,gh->nkbg", arrived[:, :, pairs:, :], screening[0], preferred_element_type=F32
    ).astype(BF16)
    blocks = jnp.einsum("nkag,nkbg->nkab", arrived[:, :, :pairs, :], screened, preferred_element_type=F32)
    blocks = blocks.reshape(blocks.shape[0], blocks.shape[1], -1).astype(BF16)
    result = lax.all_to_all(blocks, "pb", split_axis=0, concat_axis=0, tiled=True)
    return result * live.astype(BF16)[:, :, None]


def solution(mesh):
    devices = mesh.shape["pb"]

    def on_device(densities, screening, live):
        s = Sizes(densities.shape, devices)
        if s.q == devices and s.fits():
            return fast(s, densities, screening, live)
        return plain(densities, screening, live)

    in_specs = (P(None, "pb", None, None), P("pb", None, None), P(None, "pb"))
    return jax.shard_map(
        on_device, mesh=mesh, in_specs=in_specs, out_specs=P(None, "pb", None), check_vma=False
    )
```

```python
import jax
import jax.numpy as jnp
from jax import lax
from jax.experimental import pallas as pl
from jax.experimental.pallas import tpu as pltpu
from jax.sharding import PartitionSpec as P


BF16, F32 = jnp.bfloat16, jnp.float32
LANES = 128
HALF = LANES // 2
COLS = 256


VM = pl.BlockSpec(memory_space=pltpu.VMEM)
SM = pl.BlockSpec(memory_space=pltpu.SMEM)
ANY = pl.BlockSpec(memory_space=pl.ANY)
HBM = pl.BlockSpec(memory_space=pltpu.HBM)


def split(devices):
    outer = 2 ** ((devices.bit_length() - 1) // 2)
    return outer, devices // outer


class Sizes:
    def __init__(self, shape, devices):
        self.q, _, both, self.ng = shape
        self.pairs = both // 2
        self.full, self.tail = divmod(self.ng, LANES)
        self.rows = self.pairs * self.full + (self.pairs // 2 if self.tail else 0)
        self.wide = LANES * (self.full + (1 if self.tail else 0))
        self.devices = devices
        self.outer, self.inner = split(devices)

    def fits(self):
        power = self.devices & (self.devices - 1) == 0
        return power and self.inner >= 4 and self.pairs == 16 and 0 < self.tail <= HALF


def call(kernel, outs, ins, specs, scratch=(), flops=0, moved=0, after=()):
    k, a = len(ins), len(after)

    def body(*refs):
        kernel(*refs[:k], *refs[k + a :])

    return pallas(body, outs, specs, a, scratch, flops, moved)(*ins, *after)


def pallas(body, outs, specs, a, scratch, flops, moved):
    return pl.pallas_call(
        body,
        out_shape=tuple(outs),
        in_specs=[*specs, *[ANY] * a],
        out_specs=tuple(pl.BlockSpec(memory_space=pltpu.VMEM) for _ in outs),
        scratch_shapes=list(scratch),
        compiler_params=pltpu.CompilerParams(vmem_limit_bytes=24 << 20),
        cost_estimate=pl.CostEstimate(flops=flops, bytes_accessed=moved, transcendentals=0),
    )


def pack(s, read, dst, b, base):
    n = s.pairs
    for j in range(s.full):
        dst[b, base + n * j : base + n * (j + 1), :] = read(LANES * j, LANES * (j + 1))
    last = read(LANES * s.full, s.wide).astype(F32)
    lane = lax.broadcasted_iota(jnp.int32, (n // 2, LANES), 1)
    folded = jnp.where(lane < HALF, last[: n // 2], pltpu.roll(last[n // 2 :], HALF, 1))
    dst[b, base + n * s.full : base + s.rows, :] = folded.astype(BF16)


def unpack(s, src, b, base, dst, row):
    n = s.pairs
    src = src if b is None else src.at[b]
    for j in range(s.full):
        dst[row : row + n, LANES * j : LANES * (j + 1)] = src[base + n * j : base + n * (j + 1), :]
    folded = src[base + n * s.full : base + s.rows, :].astype(F32)
    last = jnp.concatenate([folded, pltpu.roll(folded, HALF, 1)], axis=0).astype(BF16)
    dst[row : row + n, LANES * s.full : s.ng] = last[:, : s.tail]


def nt(x, y):
    return lax.dot_general(x, y, (((1,), (1,)), ((), ())), preferred_element_type=F32)


def screen(s, v, w_ref, out):
    for lo in range(0, s.ng, COLS):
        hi = min(lo + COLS, s.ng)
        out[:, lo:hi] = nt(v[...], w_ref[0, lo:hi, :]).astype(BF16)


def spread(s, c, sc):
    n, count = s.pairs, c.shape[0]
    full = nt(c, sc)
    r = lax.broadcasted_iota(jnp.int32, (count, count), 0)
    k = lax.broadcasted_iota(jnp.int32, (count, count), 1)
    own = jnp.where(r // n == k // n, full, 0.0).astype(BF16)
    e = lax.broadcasted_iota(jnp.int32, (count, n * n), 0)
    f = lax.broadcasted_iota(jnp.int32, (count, n * n), 1)
    copies = jnp.where(e % n == f % n, 1.0, 0.0).astype(BF16)
    x = jnp.dot(own, copies, preferred_element_type=F32)
    return jnp.where(f // n == e % n, x, 0.0).astype(BF16)


def pick(shape, wanted):
    row = lax.broadcasted_iota(jnp.int32, shape, 0)
    column = lax.broadcasted_iota(jnp.int32, shape, 1)
    return jnp.where(wanted(row, column), 1.0, 0.0).astype(BF16)


def table(index, values):
    out = jnp.zeros_like(index)
    for i, value in enumerate(values):
        out = jnp.where(index == i, value, out)
    return out


def rows_of_pairs(s, me, offsets, c, sc):
    x = spread(s, c, sc)
    place = pick((s.devices, x.shape[0]), lambda q, r: q == (table(r // s.pairs, offsets) ^ me))
    return jnp.dot(place, x, preferred_element_type=F32)


def gather(s, me, dens, offsets, half, buf, sem):
    lo, n = (0, 2 * s.pairs) if half is None else (half * s.pairs, s.pairs)
    copies = [
        pltpu.make_async_copy(dens.at[me ^ m, 0, pl.ds(lo, n), :], buf.at[i], sem.at[i])
        for i, m in enumerate(offsets)
    ]
    for c in copies:
        c.start()
    return copies


def reader(s, ref, row, edge):
    def read(lo, hi):
        if hi <= s.ng:
            return ref[row : row + s.pairs, lo:hi]
        edge[:, : s.tail] = ref[row : row + s.pairs, lo : s.ng]
        return edge[...]

    return read


def parts_of(devices):
    outer, count = split(devices)
    inner = sorted(range(count), key=lambda p: (bin(p).count("1"), p))
    back, there = inner[: count // 2], inner[count // 2 :]
    half, most = len(there) // 2, len(back) * 3 // 4
    return [back[:most], back[most:]], [there[:half], there[half:]], list(range(outer - 1, 0, -1))


def fast(s, densities, weights, live):
    me_arr = lax.axis_index("pb").astype(jnp.int32).reshape(1)
    O, I, N, n = s.outer, s.inner, s.devices, s.pairs
    backs, (later, sooner), far = parts_of(N)
    order = [0, *far]
    back, there = backs[0] + backs[1], later + sooner
    h, g = len(back), len(later)
    T = n * n // LANES
    block = n * s.ng

    def sds(*shape):
        return jax.ShapeDtypeStruct(shape, BF16)

    def hop(x, m):
        return lax.ppermute(x, "pb", [(d, d ^ m) for d in range(N)])


    def take_v0(me_ref, dens, out, buf, edge, sem):
        offs = [far[0] * I + p for p in back]
        for i, c in enumerate(gather(s, me_ref[0], dens, offs, 1, buf, sem)):
            c.wait()
            pack(s, reader(s, buf.at[i], 0, edge.at[i]), out, i, 0)

    first = call(
        take_v0,
        [sds(h, s.rows, LANES)],
        (me_arr, pltpu.with_memory_space_constraint(densities, pltpu.HBM)),
        [SM, HBM],
        [pltpu.VMEM((h, n, s.ng), BF16), pltpu.VMEM((h, n, LANES), BF16), pltpu.SemaphoreType.DMA((h,))],
        moved=4 * h * block,
    )

    def take(picks, count, parts, after):
        def kernel(me_ref, dens, *refs):
            outs, edge = refs[: len(picks)], refs[len(picks)]
            for o, chosen in enumerate(picks):
                for i, m in enumerate(chosen):
                    ref = dens.at[me_ref[0] ^ m, 0]
                    for part in range(parts):
                        at = (o * count + i) * parts + part
                        pack(s, reader(s, ref, n * (2 - parts + part), edge.at[at]), outs[o], i, part * s.rows)

        k = len(picks) * count * parts
        return call(
            kernel,
            [sds(count, parts * s.rows, LANES)] * len(picks),
            (me_arr, densities),
            [SM, VM],
            [pltpu.VMEM((k, n, LANES), BF16)],
            moved=4 * k * block,
            after=after,
        )

    rest = take([[dz * I + p for p in back] for dz in [*far[1:], 0]], h, 1, (first[0],))
    vb = dict(zip([*far, 0], [*first, *rest]))
    vz = {dz: hop(vb[dz], dz * I) for dz in far}

    def regroup(picks, count, parts, ins, after=()):
        def kernel(*refs):
            src, outs = refs[: len(ins)], refs[len(ins) :]
            for o, chosen in zip(outs, picks):
                for i, (a, b) in enumerate(chosen):
                    o[i] = src[a][b]

        return call(
            kernel,
            [sds(count, parts * s.rows, LANES)] * len(picks),
            ins,
            [VM] * len(ins),
            moved=4 * len(picks) * count * parts * block,
            after=after,
        )

    sent = take([[dz * I + p for dz in order] for p in sooner], O, 2, (rest[0],))
    near = [hop(x, p) for x, p in zip(sent, sooner)]
    whole = take([[dz * I + p for p in later] for dz in order], g, 2, (sent[0],))
    azf = [whole[0]] + [hop(x, dz * I) for dz, x in zip(far, whole[1:])]

    zs = [vb[0]] + [vz[dz] for dz in far]
    pieces = regroup([[(zi, j) for zi in range(O)] for j in range(h)], O, 1, zs, (whole[0],))
    vin = [pieces[0]] + [hop(x, p) for x, p in zip(pieces[1:], back[1:])]

    parts = regroup([[(j, zi) for j in range(g)] for zi in range(O)], g, 2, near, (pieces[0],))
    azn = [parts[0]] + [hop(x, dz * I) for dz, x in zip(far, parts[1:])]

    def screen_back(*refs):
        src, w_ref, outs, (v, sc) = refs[:h], refs[h], refs[h + 1 : 2 * h + 1], refs[2 * h + 1 :]
        for j in range(h):
            for a in range(O):
                unpack(s, src[j], a, 0, v, n * (j * O + a))
        screen(s, v, w_ref, sc)
        for j in range(h):
            for a in range(O):
                row = n * (j * O + a)
                pack(s, lambda lo, hi, row=row: sc[row : row + n, lo:hi], outs[j], a, 0)

    m_rows = n * h * O
    sb = call(
        screen_back,
        [sds(O, s.rows, LANES)] * h,
        (*vin, weights),
        [VM] * (h + 1),
        [pltpu.VMEM((m_rows, s.ng), BF16), pltpu.VMEM((m_rows, s.wide), BF16)],
        flops=2 * m_rows * s.ng * s.ng,
        moved=2 * s.ng * s.ng,
        after=(parts[0],),
    )
    sin = [sb[0]] + [hop(x, p) for x, p in zip(sb[1:], back[1:])]
    half = len(backs[0])
    mine = regroup([[(zi, j) for zi in range(O)] for j in range(g)], O, 2, azf, (sb[0],))
    fin = [hop(x, p) for x, p in zip(mine, later)]
    out0 = regroup([[(j, zi) for j in range(half)] for zi in range(O)], half, 1, sin[:half], (mine[0],))
    sz0 = [out0[0]] + [hop(x, dz * I) for dz, x in zip(far, out0[1:])]

    def blocks_at_owner(arrived, by_outer, after):
        count, k = O * g, len(arrived)

        def kernel(*refs):
            src, w_ref, outs, (c, v, sc) = refs[:k], refs[k], refs[k + 1 : k + 1 + g], refs[k + 1 + g :]
            for zi in range(O):
                for j in range(g):
                    a, b = (zi, j) if by_outer else (j, zi)
                    unpack(s, src[a], b, 0, c, n * (zi * g + j))
                    unpack(s, src[a], b, s.rows, v, n * (zi * g + j))
            screen(s, v, w_ref, sc)
            x = spread(s, c[...], sc[:, : s.ng])
            for j in range(g):
                total = 0.0
                for t in range(T):
                    sums = pick(
                        (O * T, count * n),
                        lambda r, k, j=j, t=t: (k // n == r // T * g + j) & (r % T == t),
                    )
                    total = total + jnp.dot(
                        sums, x[:, LANES * t : LANES * (t + 1)], preferred_element_type=F32
                    )
                outs[j][...] = total

        return call(
            kernel,
            [jax.ShapeDtypeStruct((O * T, LANES), F32)] * g,
            (*arrived, weights),
            [VM] * (k + 1),
            [
                pltpu.VMEM((n * count, s.ng), BF16),
                pltpu.VMEM((n * count, s.ng), BF16),
                pltpu.VMEM((n * count, s.wide), BF16),
            ],
            flops=2 * n * count * s.ng * s.ng,
            moved=2 * s.ng * s.ng,
            after=after,
        )

    done0 = blocks_at_owner(fin, False, (out0[0],))
    done1 = blocks_at_owner(azn, True, (done0[0],))
    returned = [hop(x, p) for x, p in zip([*done0, *done1], there)]

    rows2 = len(backs[1]) * s.rows
    extra = len(there) * T

    def outward1(*refs):
        src, small, outs = refs[: h - half], refs[h - half : h - half + 2 * g], refs[h - half + 2 * g :]
        blocks = jnp.concatenate([x[...] for x in small], axis=0).astype(BF16)
        turn = pick(
            (O * extra, O * extra),
            lambda r, k: (r % T == k % T) & (r // extra == k % (O * T) // T) & (r % extra // T == k // (O * T)),
        )
        turned = jnp.dot(turn, blocks, preferred_element_type=F32)
        for zi, o in enumerate(outs):
            for j in range(h - half):
                o[s.rows * j : s.rows * (j + 1), :] = src[j][zi]
            o[rows2 : rows2 + extra, :] = turned[extra * zi : extra * (zi + 1), :].astype(BF16)

    out1 = call(
        outward1,
        [sds(rows2 + extra, LANES)] * O,
        (*sin[half:], *returned),
        [VM] * (h - half + 2 * g),
        moved=4 * O * rows2 * LANES,
    )
    sz1 = [out1[0]] + [hop(x, dz * I) for dz, x in zip(far, out1[1:])]

    def finish0(me_ref, dens, *refs):
        src, (out, c, sc) = refs[:O], refs[O:]
        for zi in range(O):
            for j in range(half):
                row = n * (zi * half + j)
                c[row : row + n, :] = dens[me_ref[0] ^ (order[zi] * I + back[j]), 0, :n, :]
                unpack(s, src[zi], j, 0, sc, row)
        out[...] = rows_of_pairs(s, me_ref[0], [dz * I + p for dz in order for p in backs[0]], c[...], sc[...])

    def finish1(me_ref, dens, *refs):
        src, (before, live_ref, out, c, sc) = refs[:O], refs[O:]
        me, k = me_ref[0], h - half
        for zi in range(O):
            for j in range(k):
                row = n * (zi * k + j)
                c[row : row + n, :] = dens[me ^ (order[zi] * I + back[half + j]), 0, :n, :]
                unpack(s, src[zi], None, s.rows * j, sc, row)
        r = rows_of_pairs(s, me, [dz * I + p for dz in order for p in backs[1]], c[...], sc[...])
        small = jnp.concatenate([x[rows2 : rows2 + extra, :].astype(F32) for x in src], axis=0).astype(BF16)
        offs = [dz * I + p for dz in order for p in there]
        placed = [
            jnp.dot(
                pick((N, O * extra), lambda q, x, t=t: (q == (table(x // T, offs) ^ me)) & (x % T == t)),
                small,
                preferred_element_type=F32,
            )
            for t in range(T)
        ]
        r = r + before[...] + jnp.concatenate(placed, axis=1)
        out[...] = (r * live_ref[...].astype(F32)).astype(BF16)

    def scratch(ps):
        return [pltpu.VMEM((n * O * len(ps), s.ng), BF16)] * 2

    partial = call(
        finish0,
        [jax.ShapeDtypeStruct((N, n * n), F32)],
        (me_arr, densities, *sz0),
        [SM] + [VM] * (1 + O),
        scratch(backs[0]),
        flops=2 * m_rows * s.ng * n,
        moved=4 * m_rows * s.ng,
        after=(out1[0],),
    )[0]
    return call(
        finish1,
        [sds(N, n * n)],
        (me_arr, densities, *sz1, partial, live),
        [SM] + [VM] * (3 + O),
        scratch(backs[1]),
        flops=2 * m_rows * s.ng * n,
        moved=4 * m_rows * s.ng,
    )[0][:, None, :]


def plain(densities, screening, live):
    pairs = densities.shape[2] // 2
    arrived = lax.all_to_all(densities, "pb", split_axis=0, concat_axis=0, tiled=True)
    screened = jnp.einsum(
        "nkbh,gh->nkbg", arrived[:, :, pairs:, :], screening[0], preferred_element_type=F32
    ).astype(BF16)
    blocks = jnp.einsum("nkag,nkbg->nkab", arrived[:, :, :pairs, :], screened, preferred_element_type=F32)
    blocks = blocks.reshape(blocks.shape[0], blocks.shape[1], -1).astype(BF16)
    result = lax.all_to_all(blocks, "pb", split_axis=0, concat_axis=0, tiled=True)
    return result * live.astype(BF16)[:, :, None]


def solution(mesh):
    devices = mesh.shape["pb"]

    def on_device(densities, screening, live):
        s = Sizes(densities.shape, devices)
        if s.q == devices and s.fits():
            return fast(s, densities, screening, live)
        return plain(densities, screening, live)

    in_specs = (P(None, "pb", None, None), P("pb", None, None), P(None, "pb"))
    return jax.shard_map(
        on_device, mesh=mesh, in_specs=in_specs, out_specs=P(None, "pb", None), check_vma=False
    )
```

```python
import jax
import jax.numpy as jnp
from jax import lax
from jax.experimental import pallas as pl
from jax.experimental.pallas import tpu as pltpu
from jax.sharding import PartitionSpec as P


STEP = 12
BF16, F32 = jnp.bfloat16, jnp.float32
LANES = 128
HALF = LANES // 2
COLS = 256


VM = pl.BlockSpec(memory_space=pltpu.VMEM)
SM = pl.BlockSpec(memory_space=pltpu.SMEM)
ANY = pl.BlockSpec(memory_space=pl.ANY)
HBM = pl.BlockSpec(memory_space=pltpu.HBM)


def split(devices):
    outer = 2 ** ((devices.bit_length() - 1) // 2)
    return outer, devices // outer


class Sizes:
    def __init__(self, shape, devices):
        self.q, _, both, self.ng = shape
        self.pairs = both // 2
        self.full, self.tail = divmod(self.ng, LANES)
        self.rows = self.pairs * self.full + (self.pairs // 2 if self.tail else 0)
        self.wide = LANES * (self.full + (1 if self.tail else 0))
        self.devices = devices
        self.outer, self.inner = split(devices)

    def fits(self):
        power = self.devices & (self.devices - 1) == 0
        return power and self.inner >= 4 and self.pairs == 16 and 0 < self.tail <= HALF


def call(kernel, outs, ins, specs, scratch=(), flops=0, moved=0, after=()):
    k, a = len(ins), len(after)

    def body(*refs):
        kernel(*refs[:k], *refs[k + a :])

    return pallas(body, outs, specs, a, scratch, flops, moved)(*ins, *after)


def pallas(body, outs, specs, a, scratch, flops, moved):
    return pl.pallas_call(
        body,
        out_shape=tuple(outs),
        in_specs=[*specs, *[ANY] * a],
        out_specs=tuple(pl.BlockSpec(memory_space=pltpu.VMEM) for _ in outs),
        scratch_shapes=list(scratch),
        compiler_params=pltpu.CompilerParams(vmem_limit_bytes=24 << 20),
        cost_estimate=pl.CostEstimate(flops=flops, bytes_accessed=moved, transcendentals=0),
    )


def pack(s, read, dst, b, base):
    n = s.pairs
    for j in range(s.full):
        dst[b, base + n * j : base + n * (j + 1), :] = read(LANES * j, LANES * (j + 1))
    last = read(LANES * s.full, s.wide).astype(F32)
    lane = lax.broadcasted_iota(jnp.int32, (n // 2, LANES), 1)
    folded = jnp.where(lane < HALF, last[: n // 2], pltpu.roll(last[n // 2 :], HALF, 1))
    dst[b, base + n * s.full : base + s.rows, :] = folded.astype(BF16)


def unpack(s, src, b, base, dst, row):
    n = s.pairs
    src = src if b is None else src.at[b]
    for j in range(s.full):
        dst[row : row + n, LANES * j : LANES * (j + 1)] = src[base + n * j : base + n * (j + 1), :]
    folded = src[base + n * s.full : base + s.rows, :].astype(F32)
    last = jnp.concatenate([folded, pltpu.roll(folded, HALF, 1)], axis=0).astype(BF16)
    dst[row : row + n, LANES * s.full : s.ng] = last[:, : s.tail]


def nt(x, y):
    return lax.dot_general(x, y, (((1,), (1,)), ((), ())), preferred_element_type=F32)


def screen(s, v, w_ref, out):
    for lo in range(0, s.ng, COLS):
        hi = min(lo + COLS, s.ng)
        out[:, lo:hi] = nt(v[...], w_ref[0, lo:hi, :]).astype(BF16)


def spread(s, c, sc):
    n, count = s.pairs, c.shape[0]
    full = nt(c, sc)
    r = lax.broadcasted_iota(jnp.int32, (count, count), 0)
    k = lax.broadcasted_iota(jnp.int32, (count, count), 1)
    own = jnp.where(r // n == k // n, full, 0.0).astype(BF16)
    e = lax.broadcasted_iota(jnp.int32, (count, n * n), 0)
    f = lax.broadcasted_iota(jnp.int32, (count, n * n), 1)
    copies = jnp.where(e % n == f % n, 1.0, 0.0).astype(BF16)
    x = jnp.dot(own, copies, preferred_element_type=F32)
    return jnp.where(f // n == e % n, x, 0.0).astype(BF16)


def pick(shape, wanted):
    row = lax.broadcasted_iota(jnp.int32, shape, 0)
    column = lax.broadcasted_iota(jnp.int32, shape, 1)
    return jnp.where(wanted(row, column), 1.0, 0.0).astype(BF16)


def table(index, values):
    out = jnp.zeros_like(index)
    for i, value in enumerate(values):
        out = jnp.where(index == i, value, out)
    return out


def rows_of_pairs(s, me, offsets, c, sc):
    x = spread(s, c, sc)
    place = pick((s.devices, x.shape[0]), lambda q, r: q == (table(r // s.pairs, offsets) ^ me))
    return jnp.dot(place, x, preferred_element_type=F32)


def gather(s, me, dens, offsets, half, buf, sem):
    lo, n = (0, 2 * s.pairs) if half is None else (half * s.pairs, s.pairs)
    copies = [
        pltpu.make_async_copy(dens.at[me ^ m, 0, pl.ds(lo, n), :], buf.at[i], sem.at[i])
        for i, m in enumerate(offsets)
    ]
    for c in copies:
        c.start()
    return copies


def reader(s, ref, row, edge):
    def read(lo, hi):
        if hi <= s.ng:
            return ref[row : row + s.pairs, lo:hi]
        edge[:, : s.tail] = ref[row : row + s.pairs, lo : s.ng]
        return edge[...]

    return read


def parts_of(devices):
    outer, count = split(devices)
    inner = sorted(range(count), key=lambda p: (bin(p).count("1"), p))
    quarter = count // 4
    low, middle = inner[:quarter] + inner[-quarter:], inner[quarter:-quarter]
    return (low, middle), (low, middle), far_of(outer)


def far_of(outer):
    return sorted(range(1, outer), key=lambda dz: (dz != outer // 2, -dz))


def fast(s, densities, weights, live):
    me_arr = lax.axis_index("pb").astype(jnp.int32).reshape(1)
    O, I, N, n = s.outer, s.inner, s.devices, s.pairs
    (out_first, in_first), (s_out, s_in), far = parts_of(N)
    order = [0, *far]
    block = n * s.ng

    def sds(*shape):
        return jax.ShapeDtypeStruct(shape, BF16)

    def hop(x, m):
        if m == 0:
            return x
        return lax.ppermute(x, "pb", [(d, d ^ m) for d in range(N)])

    def outer_hops(xs):
        return [xs[0]] + [hop(x, dz * I) for dz, x in zip(far, xs[1:])]

    def inner_hops(xs, ps):
        return [hop(x, p) for x, p in zip(xs, ps)]

    def take_v0(me_ref, dens, out, buf, edge, sem):
        offs = [far[0] * I + p for p in out_first]
        for i, c in enumerate(gather(s, me_ref[0], dens, offs, 1, buf, sem)):
            c.wait()
            pack(s, reader(s, buf.at[i], 0, edge.at[i]), out, i, 0)

    k = len(out_first)
    first = call(
        take_v0,
        [sds(k, s.rows, LANES)],
        (me_arr, pltpu.with_memory_space_constraint(densities, pltpu.HBM)),
        [SM, HBM],
        [pltpu.VMEM((k, n, s.ng), BF16), pltpu.VMEM((k, n, LANES), BF16), pltpu.SemaphoreType.DMA((k,))],
        moved=4 * k * block,
    )

    def take(picks, after):
        count = len(picks[0])

        def kernel(me_ref, dens, *refs):
            outs, edge = refs[: len(picks)], refs[len(picks)]
            for o, chosen in enumerate(picks):
                for i, m in enumerate(chosen):
                    pack(s, reader(s, dens.at[me_ref[0] ^ m, 0], n, edge.at[o * count + i]), outs[o], i, 0)

        return call(
            kernel,
            [sds(count, s.rows, LANES)] * len(picks),
            (me_arr, densities),
            [SM, VM],
            [pltpu.VMEM((len(picks) * count, n, LANES), BF16)],
            moved=4 * len(picks) * count * block,
            after=after,
        )

    def turn(ins, after=()):
        count = ins[0].shape[0]

        def kernel(*refs):
            src, outs = refs[: len(ins)], refs[len(ins) :]
            for i, o in enumerate(outs):
                for j, x in enumerate(src):
                    o[j] = x[i]

        return call(
            kernel,
            [sds(len(ins), s.rows, LANES)] * count,
            ins,
            [VM] * len(ins),
            moved=4 * len(ins) * count * block,
            after=after,
        )

    sent = take([[dz * I + p for dz in order] for p in in_first], (first[0],))
    near = inner_hops(sent, in_first)
    rest = take([[dz * I + p for p in out_first] for dz in [*far[1:], 0]], (sent[0],))
    vz = outer_hops([rest[-1], *first, *rest[:-1]])
    wz = outer_hops(turn(near, (rest[0],)))
    pieces = turn(vz, (wz[0],))
    vin = inner_hops(pieces, out_first)

    def screened(ins, picks, shapes, after):
        rows = n * len(picks)

        def kernel(*refs):
            src, w_ref, outs, (v, sc) = refs[: len(ins)], refs[len(ins)], refs[len(ins) + 1 : -2], refs[-2:]
            for x, (a, b, _, _) in enumerate(picks):
                unpack(s, src[a], b, 0, v, n * x)
            screen(s, v, w_ref, sc)
            for x, (_, _, o, i) in enumerate(picks):
                pack(s, lambda lo, hi, row=n * x: sc[row : row + n, lo:hi], outs[o], i, 0)

        return call(
            kernel,
            [sds(count, s.rows, LANES) for count in shapes],
            (*ins, weights),
            [VM] * (len(ins) + 1),
            [pltpu.VMEM((rows, s.ng), BF16), pltpu.VMEM((rows, s.wide), BF16)],
            flops=2 * rows * s.ng * s.ng,
            moved=2 * s.ng * s.ng,
            after=after,
        )

    low, extra = len(s_out), out_first[len(s_out) :]
    picks = [(j, zi, zi, j) for j in range(low) for zi in range(O)]
    picks += [(low + j, zi, O + j, zi) for j in range(len(extra)) for zi in range(O)]
    made = screened(vin, picks, [low] * O + [O] * len(extra), (pieces[0],))
    s1z = outer_hops(made[:O])
    early = inner_hops(made[O:], extra)
    count = len(in_first)
    picks = [(zi, j, j, zi) for j in range(count) for zi in range(O)]
    made = screened(wz, picks, [O] * count, (made[0],))
    sin = early + inner_hops(made, in_first)
    s2z = outer_hops(turn(sin))
    fin = inner_hops(turn(s1z, (s2z[0],)), s_out)

    def finish(ins, picks, others, after=()):
        rows, last = n * len(picks), len(others) > 0

        def kernel(me_ref, dens, *refs):
            src, more, (out, c, sc) = refs[: len(ins)], refs[len(ins) : -3], refs[-3:]
            me = me_ref[0]
            for x, (a, b, m) in enumerate(picks):
                c[n * x : n * (x + 1), :] = dens[me ^ m, 0, :n, :]
                unpack(s, src[a], b, 0, sc, n * x)
            r, step = 0.0, STEP * n
            for lo in range(0, rows, step):
                hi = min(lo + step, rows)
                offs = [m for _, _, m in picks[lo // n : hi // n]]
                r = r + rows_of_pairs(s, me, offs, c[lo:hi, :], sc[lo:hi, :])
            if last:
                before, live_ref = more
                out[...] = ((r + before[...]) * live_ref[...].astype(F32)).astype(BF16)
            else:
                out[...] = r

        return call(
            kernel,
            [jax.ShapeDtypeStruct((N, n * n), BF16 if last else F32)],
            (me_arr, densities, *ins, *others),
            [SM] + [VM] * (1 + len(ins) + len(others)),
            [pltpu.VMEM((rows, s.ng), BF16)] * 2,
            flops=2 * rows * s.ng * n,
            moved=4 * rows * s.ng,
            after=after,
        )[0]

    picks = [(j, zi, dz * I + p) for j, p in enumerate(s_out) for zi, dz in enumerate(order)]
    picks += [(len(s_out), j, p) for j, p in enumerate(s_in)]
    partial = finish([*fin, s2z[0]], picks, ())
    picks = [(zi, j, dz * I + p) for zi, dz in enumerate(far) for j, p in enumerate(s_in)]
    return finish(s2z[1:], picks, (partial, live))[:, None, :]


def plain(densities, screening, live):
    pairs = densities.shape[2] // 2
    arrived = lax.all_to_all(densities, "pb", split_axis=0, concat_axis=0, tiled=True)
    screened = jnp.einsum(
        "nkbh,gh->nkbg", arrived[:, :, pairs:, :], screening[0], preferred_element_type=F32
    ).astype(BF16)
    blocks = jnp.einsum("nkag,nkbg->nkab", arrived[:, :, :pairs, :], screened, preferred_element_type=F32)
    blocks = blocks.reshape(blocks.shape[0], blocks.shape[1], -1).astype(BF16)
    result = lax.all_to_all(blocks, "pb", split_axis=0, concat_axis=0, tiled=True)
    return result * live.astype(BF16)[:, :, None]


def solution(mesh):
    devices = mesh.shape["pb"]

    def on_device(densities, screening, live):
        s = Sizes(densities.shape, devices)
        if s.q == devices and s.fits():
            return fast(s, densities, screening, live)
        return plain(densities, screening, live)

    in_specs = (P(None, "pb", None, None), P("pb", None, None), P(None, "pb"))
    return jax.shard_map(
        on_device, mesh=mesh, in_specs=in_specs, out_specs=P(None, "pb", None), check_vma=False
    )
```

```python
import jax
import jax.numpy as jnp
from jax import lax
from jax.experimental import pallas as pl
from jax.experimental.pallas import tpu as pltpu
from jax.sharding import PartitionSpec as P


STEP = 12
BF16, F32 = jnp.bfloat16, jnp.float32
LANES = 128
HALF = LANES // 2
COLS = 256


VM = pl.BlockSpec(memory_space=pltpu.VMEM)
SM = pl.BlockSpec(memory_space=pltpu.SMEM)
ANY = pl.BlockSpec(memory_space=pl.ANY)
HBM = pl.BlockSpec(memory_space=pltpu.HBM)


def split(devices):
    outer = 2 ** ((devices.bit_length() - 1) // 2)
    return outer, devices // outer


class Sizes:
    def __init__(self, shape, devices):
        self.q, _, both, self.ng = shape
        self.pairs = both // 2
        self.full, self.tail = divmod(self.ng, LANES)
        self.rows = self.pairs * self.full + (self.pairs // 2 if self.tail else 0)
        self.wide = LANES * (self.full + (1 if self.tail else 0))
        self.devices = devices
        self.outer, self.inner = split(devices)

    def fits(self):
        power = self.devices & (self.devices - 1) == 0
        return power and self.inner >= 4 and self.pairs == 16 and 0 < self.tail <= HALF


def call(kernel, outs, ins, specs, scratch=(), flops=0, moved=0, after=()):
    k, a = len(ins), len(after)

    def body(*refs):
        kernel(*refs[:k], *refs[k + a :])

    return pallas(body, outs, specs, a, scratch, flops, moved)(*ins, *after)


def pallas(body, outs, specs, a, scratch, flops, moved):
    return pl.pallas_call(
        body,
        out_shape=tuple(outs),
        in_specs=[*specs, *[ANY] * a],
        out_specs=tuple(pl.BlockSpec(memory_space=pltpu.VMEM) for _ in outs),
        scratch_shapes=list(scratch),
        compiler_params=pltpu.CompilerParams(vmem_limit_bytes=24 << 20),
        cost_estimate=pl.CostEstimate(flops=flops, bytes_accessed=moved, transcendentals=0),
    )


def pack(s, read, dst, b, base):
    n = s.pairs
    for j in range(s.full):
        dst[b, base + n * j : base + n * (j + 1), :] = read(LANES * j, LANES * (j + 1))
    last = read(LANES * s.full, s.wide).astype(F32)
    lane = lax.broadcasted_iota(jnp.int32, (n // 2, LANES), 1)
    folded = jnp.where(lane < HALF, last[: n // 2], pltpu.roll(last[n // 2 :], HALF, 1))
    dst[b, base + n * s.full : base + s.rows, :] = folded.astype(BF16)


def unpack(s, src, b, base, dst, row):
    n = s.pairs
    src = src if b is None else src.at[b]
    for j in range(s.full):
        dst[row : row + n, LANES * j : LANES * (j + 1)] = src[base + n * j : base + n * (j + 1), :]
    folded = src[base + n * s.full : base + s.rows, :].astype(F32)
    last = jnp.concatenate([folded, pltpu.roll(folded, HALF, 1)], axis=0).astype(BF16)
    dst[row : row + n, LANES * s.full : s.ng] = last[:, : s.tail]


def nt(x, y):
    return lax.dot_general(x, y, (((1,), (1,)), ((), ())), preferred_element_type=F32)


def screen(s, v, w_ref, out):
    for lo in range(0, s.ng, COLS):
        hi = min(lo + COLS, s.ng)
        out[:, lo:hi] = nt(v[...], w_ref[0, lo:hi, :]).astype(BF16)


def spread(s, c, sc):
    n, count = s.pairs, c.shape[0]
    full = nt(c, sc)
    r = lax.broadcasted_iota(jnp.int32, (count, count), 0)
    k = lax.broadcasted_iota(jnp.int32, (count, count), 1)
    own = jnp.where(r // n == k // n, full, 0.0).astype(BF16)
    e = lax.broadcasted_iota(jnp.int32, (count, n * n), 0)
    f = lax.broadcasted_iota(jnp.int32, (count, n * n), 1)
    copies = jnp.where(e % n == f % n, 1.0, 0.0).astype(BF16)
    x = jnp.dot(own, copies, preferred_element_type=F32)
    return jnp.where(f // n == e % n, x, 0.0).astype(BF16)


def pick(shape, wanted):
    row = lax.broadcasted_iota(jnp.int32, shape, 0)
    column = lax.broadcasted_iota(jnp.int32, shape, 1)
    return jnp.where(wanted(row, column), 1.0, 0.0).astype(BF16)


def table(index, values):
    out = jnp.zeros_like(index)
    for i, value in enumerate(values):
        out = jnp.where(index == i, value, out)
    return out


def rows_of_pairs(s, me, offsets, c, sc):
    x = spread(s, c, sc)
    place = pick((s.devices, x.shape[0]), lambda q, r: q == (table(r // s.pairs, offsets) ^ me))
    return jnp.dot(place, x, preferred_element_type=F32)


def gather(s, me, dens, offsets, half, buf, sem):
    lo, n = (0, 2 * s.pairs) if half is None else (half * s.pairs, s.pairs)
    copies = [
        pltpu.make_async_copy(dens.at[me ^ m, 0, pl.ds(lo, n), :], buf.at[i], sem.at[i])
        for i, m in enumerate(offsets)
    ]
    for c in copies:
        c.start()
    return copies


def reader(s, ref, row, edge):
    def read(lo, hi):
        if hi <= s.ng:
            return ref[row : row + s.pairs, lo:hi]
        edge[:, : s.tail] = ref[row : row + s.pairs, lo : s.ng]
        return edge[...]

    return read


def parts_of(devices):
    outer, count = split(devices)
    inner = sorted(range(count), key=lambda p: (bin(p).count("1"), p))
    quarter = count // 4
    low, middle = inner[:quarter] + inner[-quarter:], inner[quarter:-quarter]
    return (low, middle), (low, middle), far_of(outer)


def far_of(outer):
    return sorted(range(1, outer), key=lambda dz: (dz != outer // 2, -dz))


def fast(s, densities, weights, live):
    me_arr = lax.axis_index("pb").astype(jnp.int32).reshape(1)
    O, I, N, n = s.outer, s.inner, s.devices, s.pairs
    (out_first, in_first), (s_out, s_in), far = parts_of(N)
    order = [0, *far]
    block = n * s.ng

    def sds(*shape):
        return jax.ShapeDtypeStruct(shape, BF16)

    def hop(x, m):
        if m == 0:
            return x
        return lax.ppermute(x, "pb", [(d, d ^ m) for d in range(N)])

    def outer_hops(xs):
        return [xs[0]] + [hop(x, dz * I) for dz, x in zip(far, xs[1:])]

    def inner_hops(xs, ps):
        return [hop(x, p) for x, p in zip(xs, ps)]

    def take_v0(me_ref, dens, out, buf, edge, sem):
        offs = [far[0] * I + p for p in out_first]
        for i, c in enumerate(gather(s, me_ref[0], dens, offs, 1, buf, sem)):
            c.wait()
            pack(s, reader(s, buf.at[i], 0, edge.at[i]), out, i, 0)

    k = len(out_first)
    first = call(
        take_v0,
        [sds(k, s.rows, LANES)],
        (me_arr, pltpu.with_memory_space_constraint(densities, pltpu.HBM)),
        [SM, HBM],
        [pltpu.VMEM((k, n, s.ng), BF16), pltpu.VMEM((k, n, LANES), BF16), pltpu.SemaphoreType.DMA((k,))],
        moved=4 * k * block,
    )

    def take(picks, after):
        count = len(picks[0])

        def kernel(me_ref, dens, *refs):
            outs, edge = refs[: len(picks)], refs[len(picks)]
            for o, chosen in enumerate(picks):
                for i, m in enumerate(chosen):
                    pack(s, reader(s, dens.at[me_ref[0] ^ m, 0], n, edge.at[o * count + i]), outs[o], i, 0)

        return call(
            kernel,
            [sds(count, s.rows, LANES)] * len(picks),
            (me_arr, densities),
            [SM, VM],
            [pltpu.VMEM((len(picks) * count, n, LANES), BF16)],
            moved=4 * len(picks) * count * block,
            after=after,
        )

    def turn(ins, after=()):
        count = ins[0].shape[0]

        def kernel(*refs):
            src, outs = refs[: len(ins)], refs[len(ins) :]
            for i, o in enumerate(outs):
                for j, x in enumerate(src):
                    o[j] = x[i]

        return call(
            kernel,
            [sds(len(ins), s.rows, LANES)] * count,
            ins,
            [VM] * len(ins),
            moved=4 * len(ins) * count * block,
            after=after,
        )

    sent = take([[dz * I + p for dz in order] for p in in_first], (first[0],))
    near = inner_hops(sent, in_first)
    rest = take([[dz * I + p for p in out_first] for dz in [*far[1:], 0]], (sent[0],))
    vz = outer_hops([rest[-1], *first, *rest[:-1]])
    wz = outer_hops(turn(near, (rest[0],)))
    pieces = turn(vz, (wz[0],))
    vin = inner_hops(pieces, out_first)

    def screened(ins, picks, shapes, after):
        rows = n * len(picks)

        def kernel(*refs):
            src, w_ref, outs, (v, sc) = refs[: len(ins)], refs[len(ins)], refs[len(ins) + 1 : -2], refs[-2:]
            for x, (a, b, _, _) in enumerate(picks):
                unpack(s, src[a], b, 0, v, n * x)
            screen(s, v, w_ref, sc)
            for x, (_, _, o, i) in enumerate(picks):
                pack(s, lambda lo, hi, row=n * x: sc[row : row + n, lo:hi], outs[o], i, 0)

        return call(
            kernel,
            [sds(count, s.rows, LANES) for count in shapes],
            (*ins, weights),
            [VM] * (len(ins) + 1),
            [pltpu.VMEM((rows, s.ng), BF16), pltpu.VMEM((rows, s.wide), BF16)],
            flops=2 * rows * s.ng * s.ng,
            moved=2 * s.ng * s.ng,
            after=after,
        )

    low, extra = len(s_out), out_first[len(s_out) :]
    picks = [(j, zi, zi, j) for j in range(low) for zi in range(O)]
    picks += [(low + j, zi, O + j, zi) for j in range(len(extra)) for zi in range(O)]
    made = screened(vin, picks, [low] * O + [O] * len(extra), (pieces[0],))
    s1z = outer_hops(made[:O])
    early = inner_hops(made[O:], extra)
    count = len(in_first)
    picks = [(zi, j, j, zi) for j in range(count) for zi in range(O)]
    made = screened(wz, picks, [O] * count, (made[0],))
    sin = early + inner_hops(made, in_first)
    s2z = outer_hops(turn(sin))
    fin = inner_hops(turn(s1z, (s2z[0],)), s_out)

    def finish(ins, picks, others, after=()):
        rows, last = n * len(picks), len(others) > 0

        def kernel(me_ref, dens, *refs):
            src, more, (out, c, sc) = refs[: len(ins)], refs[len(ins) : -3], refs[-3:]
            me = me_ref[0]
            for x, (a, b, m) in enumerate(picks):
                c[n * x : n * (x + 1), :] = dens[me ^ m, 0, :n, :]
                unpack(s, src[a], b, 0, sc, n * x)
            r, step = 0.0, STEP * n
            for lo in range(0, rows, step):
                hi = min(lo + step, rows)
                offs = [m for _, _, m in picks[lo // n : hi // n]]
                r = r + rows_of_pairs(s, me, offs, c[lo:hi, :], sc[lo:hi, :])
            if last:
                before, live_ref = more
                alive = pick((N, N), lambda q, k: q == k).astype(F32) * live_ref[...].astype(F32)
                out[...] = ((r + before[...]) * jnp.sum(alive, axis=1, keepdims=True)).astype(BF16)
            else:
                out[...] = r

        return call(
            kernel,
            [jax.ShapeDtypeStruct((N, n * n), BF16 if last else F32)],
            (me_arr, densities, *ins, *others),
            [SM] + [VM] * (1 + len(ins) + len(others)),
            [pltpu.VMEM((rows, s.ng), BF16)] * 2,
            flops=2 * rows * s.ng * n,
            moved=4 * rows * s.ng,
            after=after,
        )[0]

    picks = [(j, zi, dz * I + p) for j, p in enumerate(s_out) for zi, dz in enumerate(order)]
    picks += [(len(s_out), j, p) for j, p in enumerate(s_in)]
    partial = finish([*fin, s2z[0]], picks, ())
    picks = [(zi, j, dz * I + p) for zi, dz in enumerate(far) for j, p in enumerate(s_in)]
    return finish(s2z[1:], picks, (partial, live.T))[:, None, :]


def plain(densities, screening, live):
    pairs = densities.shape[2] // 2
    arrived = lax.all_to_all(densities, "pb", split_axis=0, concat_axis=0, tiled=True)
    screened = jnp.einsum(
        "nkbh,gh->nkbg", arrived[:, :, pairs:, :], screening[0], preferred_element_type=F32
    ).astype(BF16)
    blocks = jnp.einsum("nkag,nkbg->nkab", arrived[:, :, :pairs, :], screened, preferred_element_type=F32)
    blocks = blocks.reshape(blocks.shape[0], blocks.shape[1], -1).astype(BF16)
    result = lax.all_to_all(blocks, "pb", split_axis=0, concat_axis=0, tiled=True)
    return result * live.astype(BF16)[:, :, None]


def solution(mesh):
    devices = mesh.shape["pb"]

    def on_device(densities, screening, live):
        s = Sizes(densities.shape, devices)
        if s.q == devices and s.fits():
            return fast(s, densities, screening, live)
        return plain(densities, screening, live)

    in_specs = (P(None, "pb", None, None), P("pb", None, None), P(None, "pb"))
    return jax.shard_map(
        on_device, mesh=mesh, in_specs=in_specs, out_specs=P(None, "pb", None), check_vma=False
    )
```

```python
import jax
import jax.numpy as jnp
from jax import lax
from jax.experimental import pallas as pl
from jax.experimental.pallas import tpu as pltpu
from jax.sharding import PartitionSpec as P


STEP = 12
BF16, F32 = jnp.bfloat16, jnp.float32
LANES = 128
SUBLANES = 8
QUAD = 4
PART = LANES // QUAD
EIGHTH = PART // 2
COLS = 256


VM = pl.BlockSpec(memory_space=pltpu.VMEM)
SM = pl.BlockSpec(memory_space=pltpu.SMEM)
ANY = pl.BlockSpec(memory_space=pl.ANY)
HBM = pl.BlockSpec(memory_space=pltpu.HBM)


def split(devices):
    outer = 2 ** ((devices.bit_length() - 1) // 2)
    return outer, devices // outer


class Sizes:
    def __init__(self, shape, devices):
        self.q, _, both, self.ng = shape
        self.pairs = both // 2
        self.full, self.tail = divmod(self.ng, LANES)
        self.body = self.pairs * self.full
        self.wide = LANES * (self.full + (1 if self.tail else 0))
        self.devices = devices
        self.outer, self.inner = split(devices)

    def fits(self):
        power = self.devices & (self.devices - 1) == 0
        grouped = self.outer % QUAD == 0 and self.inner % (2 * QUAD) == 0
        return power and grouped and self.pairs == 16 and 8 * self.tail == 3 * LANES

    def packed(self, count):
        return count * self.body + count // QUAD * 3 * SUBLANES


def call(kernel, outs, ins, specs, scratch=(), flops=0, moved=0, after=()):
    k, a = len(ins), len(after)

    def body(*refs):
        kernel(*refs[:k], *refs[k + a :])

    return pallas(body, outs, specs, a, scratch, flops, moved)(*ins, *after)


def pallas(body, outs, specs, a, scratch, flops, moved):
    return pl.pallas_call(
        body,
        out_shape=tuple(outs),
        in_specs=[*specs, *[ANY] * a],
        out_specs=tuple(pl.BlockSpec(memory_space=pltpu.VMEM) for _ in outs),
        scratch_shapes=list(scratch),
        compiler_params=pltpu.CompilerParams(vmem_limit_bytes=24 << 20),
        cost_estimate=pl.CostEstimate(flops=flops, bytes_accessed=moved, transcendentals=0),
    )


def pack(s, reads, dst):
    n, count = s.pairs, len(reads)
    for b, read in enumerate(reads):
        for j in range(s.full):
            at = s.body * b + n * j
            dst[at : at + n, :] = read(LANES * j, LANES * (j + 1))
    lane = lax.broadcasted_iota(jnp.int32, (SUBLANES, LANES), 1)
    for quad in range(count // QUAD):
        pieces = []
        for read in reads[QUAD * quad : QUAD * (quad + 1)]:
            last = read(LANES * s.full, s.wide).astype(F32)
            pieces += [last[:SUBLANES], last[SUBLANES:]]
        tiles = []
        for tile in range(2):
            out = pieces[QUAD * tile]
            for k in range(1, QUAD):
                out = jnp.where(lane < PART * k, out, pltpu.roll(pieces[QUAD * tile + k], PART * k, 1))
            tiles.append(out)
        out = pltpu.roll(pieces[0], LANES - PART, 1)
        for k in range(1, 2 * QUAD):
            out = jnp.where(lane < EIGHTH * k, out, pltpu.roll(pieces[k], (EIGHTH * k - PART) % LANES, 1))
        tiles.append(out)
        for i, tile in enumerate(tiles):
            at = s.body * count + SUBLANES * (3 * quad + i)
            dst[at : at + SUBLANES, :] = tile.astype(BF16)


def last_columns(s, src, b, count):
    lane = lax.broadcasted_iota(jnp.int32, (SUBLANES, LANES), 1)
    at = s.body * count + SUBLANES * 3 * (b // QUAD)
    halves = []
    for k in (2 * (b % QUAD), 2 * (b % QUAD) + 1):
        main = at + SUBLANES * (k // QUAD)
        x = pltpu.roll(src[main : main + SUBLANES, :].astype(F32), (LANES - PART * (k % QUAD)) % LANES, 1)
        y = src[at + 2 * SUBLANES : at + 3 * SUBLANES, :].astype(F32)
        halves.append(jnp.where(lane < PART, x, pltpu.roll(y, (PART - EIGHTH * k) % LANES, 1)))
    return jnp.concatenate(halves, axis=0).astype(BF16)


def unpack(s, src, b, count, dst, row):
    n = s.pairs
    for j in range(s.full):
        at = s.body * b + n * j
        dst[row : row + n, LANES * j : LANES * (j + 1)] = src[at : at + n, :]
    dst[row : row + n, LANES * s.full : s.ng] = last_columns(s, src, b, count)[:, : s.tail]


def packed_reader(s, src, b, count):
    def read(lo, hi):
        if hi <= LANES * s.full:
            at = s.body * b + s.pairs * (lo // LANES)
            return src[at : at + s.pairs, :]
        return last_columns(s, src, b, count)

    return read


def nt(x, y):
    return lax.dot_general(x, y, (((1,), (1,)), ((), ())), preferred_element_type=F32)


def screen(s, v, w_ref, out):
    for lo in range(0, s.ng, COLS):
        hi = min(lo + COLS, s.ng)
        out[:, lo:hi] = nt(v[...], w_ref[0, lo:hi, :]).astype(BF16)


def spread(s, c, sc):
    n, count = s.pairs, c.shape[0]
    full = nt(c, sc)
    r = lax.broadcasted_iota(jnp.int32, (count, count), 0)
    k = lax.broadcasted_iota(jnp.int32, (count, count), 1)
    own = jnp.where(r // n == k // n, full, 0.0).astype(BF16)
    e = lax.broadcasted_iota(jnp.int32, (count, n * n), 0)
    f = lax.broadcasted_iota(jnp.int32, (count, n * n), 1)
    copies = jnp.where(e % n == f % n, 1.0, 0.0).astype(BF16)
    x = jnp.dot(own, copies, preferred_element_type=F32)
    return jnp.where(f // n == e % n, x, 0.0).astype(BF16)


def pick(shape, wanted):
    row = lax.broadcasted_iota(jnp.int32, shape, 0)
    column = lax.broadcasted_iota(jnp.int32, shape, 1)
    return jnp.where(wanted(row, column), 1.0, 0.0).astype(BF16)


def table(index, values):
    out = jnp.zeros_like(index)
    for i, value in enumerate(values):
        out = jnp.where(index == i, value, out)
    return out


def rows_of_pairs(s, me, offsets, c, sc):
    x = spread(s, c, sc)
    place = pick((s.devices, x.shape[0]), lambda q, r: q == (table(r // s.pairs, offsets) ^ me))
    return jnp.dot(place, x, preferred_element_type=F32)


def gather(s, me, dens, offsets, half, buf, sem):
    lo, n = (0, 2 * s.pairs) if half is None else (half * s.pairs, s.pairs)
    copies = [
        pltpu.make_async_copy(dens.at[me ^ m, 0, pl.ds(lo, n), :], buf.at[i], sem.at[i])
        for i, m in enumerate(offsets)
    ]
    for c in copies:
        c.start()
    return copies


def reader(s, ref, row, edge):
    def read(lo, hi):
        if hi <= s.ng:
            return ref[row : row + s.pairs, lo:hi]
        edge[:, : s.tail] = ref[row : row + s.pairs, lo : s.ng]
        return edge[...]

    return read


def parts_of(devices):
    outer, count = split(devices)
    inner = sorted(range(count), key=lambda p: (bin(p).count("1"), p))
    quarter = count // 4
    low, middle = inner[:quarter] + inner[-quarter:], inner[quarter:-quarter]
    return (low, middle), (low, middle), far_of(outer)


def far_of(outer):
    return sorted(range(1, outer), key=lambda dz: (dz != outer // 2, -dz))


def fast(s, densities, weights, live):
    me_arr = lax.axis_index("pb").astype(jnp.int32).reshape(1)
    O, I, N, n = s.outer, s.inner, s.devices, s.pairs
    (out_first, in_first), (s_out, s_in), far = parts_of(N)
    order = [0, *far]
    block = n * s.ng

    def sds(*shape):
        return jax.ShapeDtypeStruct(shape, BF16)

    def hop(x, m):
        if m == 0:
            return x
        return lax.ppermute(x, "pb", [(d, d ^ m) for d in range(N)])

    def outer_hops(xs):
        return [xs[0]] + [hop(x, dz * I) for dz, x in zip(far, xs[1:])]

    def inner_hops(xs, ps):
        return [hop(x, p) for x, p in zip(xs, ps)]

    def take_v0(me_ref, dens, out, buf, edge, sem):
        offs = [far[0] * I + p for p in out_first]
        for c in gather(s, me_ref[0], dens, offs, 1, buf, sem):
            c.wait()
        pack(s, [reader(s, buf.at[i], 0, edge.at[i]) for i in range(k)], out)

    k = len(out_first)
    first = call(
        take_v0,
        [sds(s.packed(k), LANES)],
        (me_arr, pltpu.with_memory_space_constraint(densities, pltpu.HBM)),
        [SM, HBM],
        [pltpu.VMEM((k, n, s.ng), BF16), pltpu.VMEM((k, n, LANES), BF16), pltpu.SemaphoreType.DMA((k,))],
        moved=4 * k * block,
    )

    def take(picks, after):
        count = len(picks[0])

        def kernel(me_ref, dens, *refs):
            outs, edge = refs[: len(picks)], refs[len(picks)]
            for o, chosen in enumerate(picks):
                reads = [
                    reader(s, dens.at[me_ref[0] ^ m, 0], n, edge.at[o * count + i])
                    for i, m in enumerate(chosen)
                ]
                pack(s, reads, outs[o])

        return call(
            kernel,
            [sds(s.packed(count), LANES)] * len(picks),
            (me_arr, densities),
            [SM, VM],
            [pltpu.VMEM((len(picks) * count, n, LANES), BF16)],
            moved=4 * len(picks) * count * block,
            after=after,
        )

    def turn(ins, count, after=()):
        def kernel(*refs):
            src, outs = refs[: len(ins)], refs[len(ins) :]
            for i, o in enumerate(outs):
                pack(s, [packed_reader(s, x, i, count) for x in src], o)

        return call(
            kernel,
            [sds(s.packed(len(ins)), LANES)] * count,
            ins,
            [VM] * len(ins),
            moved=4 * len(ins) * count * block,
            after=after,
        )

    sent = take([[dz * I + p for dz in order] for p in in_first], (first[0],))
    near = inner_hops(sent, in_first)
    rest = take([[dz * I + p for p in out_first] for dz in [*far[1:], 0]], (sent[0],))
    vz = outer_hops([rest[-1], *first, *rest[:-1]])
    wz = outer_hops(turn(near, O, (rest[0],)))
    pieces = turn(vz, len(out_first), (wz[0],))
    vin = inner_hops(pieces, out_first)

    def screened(ins, held, picks, shapes, after):
        rows = n * len(picks)

        def kernel(*refs):
            src, w_ref, outs, (v, sc) = refs[: len(ins)], refs[len(ins)], refs[len(ins) + 1 : -2], refs[-2:]
            for x, (a, b, _, _) in enumerate(picks):
                unpack(s, src[a], b, held, v, n * x)
            screen(s, v, w_ref, sc)
            for o, count in enumerate(shapes):
                reads = [None] * count
                for x, (_, _, to, i) in enumerate(picks):
                    if to == o:
                        reads[i] = lambda lo, hi, row=n * x: sc[row : row + n, lo:hi]
                pack(s, reads, outs[o])

        return call(
            kernel,
            [sds(s.packed(count), LANES) for count in shapes],
            (*ins, weights),
            [VM] * (len(ins) + 1),
            [pltpu.VMEM((rows, s.ng), BF16), pltpu.VMEM((rows, s.wide), BF16)],
            flops=2 * rows * s.ng * s.ng,
            moved=2 * s.ng * s.ng,
            after=after,
        )

    low, extra = len(s_out), out_first[len(s_out) :]
    picks = [(j, zi, zi, j) for j in range(low) for zi in range(O)]
    picks += [(low + j, zi, O + j, zi) for j in range(len(extra)) for zi in range(O)]
    made = screened(vin, O, picks, [low] * O + [O] * len(extra), (pieces[0],))
    s1z = outer_hops(made[:O])
    early = inner_hops(made[O:], extra)
    count = len(in_first)
    picks = [(zi, j, j, zi) for j in range(count) for zi in range(O)]
    made = screened(wz, count, picks, [O] * count, (made[0],))
    sin = early + inner_hops(made, in_first)
    s2z = outer_hops(turn(sin, O))
    fin = inner_hops(turn(s1z, len(s_out), (s2z[0],)), s_out)

    def finish(ins, held, picks, others, after=()):
        rows, last = n * len(picks), len(others) > 1

        def kernel(me_ref, dens, *refs):
            src, more, (out, c, sc) = refs[: len(ins)], refs[len(ins) : -3], refs[-3:]
            me = me_ref[0]
            for x, (a, b, m) in enumerate(picks):
                c[n * x : n * (x + 1), :] = dens[me ^ m, 0, :n, :]
                unpack(s, src[a], b, held[a], sc, n * x)
            r, step = 0.0, STEP * n
            for lo in range(0, rows, step):
                hi = min(lo + step, rows)
                offs = [m for _, _, m in picks[lo // n : hi // n]]
                r = r + rows_of_pairs(s, me, offs, c[lo:hi, :], sc[lo:hi, :])
            if last:
                before, live_ref = more
                alive = pick((N, N), lambda q, k: q == k).astype(F32) * live_ref[...].astype(F32)
                out[...] = ((r + before[...]) * jnp.sum(alive, axis=1, keepdims=True)).astype(BF16)
            else:
                out[...] = r + more[0][...] if more else r

        return call(
            kernel,
            [jax.ShapeDtypeStruct((N, n * n), BF16 if last else F32)],
            (me_arr, densities, *ins, *others),
            [SM] + [VM] * (1 + len(ins) + len(others)),
            [pltpu.VMEM((rows, s.ng), BF16)] * 2,
            flops=2 * rows * s.ng * n,
            moved=4 * rows * s.ng,
            after=after,
        )[0]

    def plane_picks(ps):
        return [(j, zi, dz * I + p) for j, p in enumerate(ps) for zi, dz in enumerate(order)]

    few = sum(p < 2 for p in s_out)
    picks = plane_picks(s_out[:few]) + [(few, j, p) for j, p in enumerate(s_in)]
    total = finish([*fin[:few], s2z[0]], [O] * few + [len(s_in)], picks, ())
    total = finish(fin[few:], [O] * (len(fin) - few), plane_picks(s_out[few:]), (total,))
    picks = [(a, j, dz * I + p) for a, dz in enumerate(far) for j, p in enumerate(s_in)]
    out = finish(s2z[1:], [len(s_in)] * len(far), picks, (total, live.T))
    return out[:, None, :]


def plain(densities, screening, live):
    pairs = densities.shape[2] // 2
    arrived = lax.all_to_all(densities, "pb", split_axis=0, concat_axis=0, tiled=True)
    screened = jnp.einsum(
        "nkbh,gh->nkbg", arrived[:, :, pairs:, :], screening[0], preferred_element_type=F32
    ).astype(BF16)
    blocks = jnp.einsum("nkag,nkbg->nkab", arrived[:, :, :pairs, :], screened, preferred_element_type=F32)
    blocks = blocks.reshape(blocks.shape[0], blocks.shape[1], -1).astype(BF16)
    result = lax.all_to_all(blocks, "pb", split_axis=0, concat_axis=0, tiled=True)
    return result * live.astype(BF16)[:, :, None]


def solution(mesh):
    devices = mesh.shape["pb"]

    def on_device(densities, screening, live):
        s = Sizes(densities.shape, devices)
        if s.q == devices and s.fits():
            return fast(s, densities, screening, live)
        return plain(densities, screening, live)

    in_specs = (P(None, "pb", None, None), P("pb", None, None), P(None, "pb"))
    return jax.shard_map(
        on_device, mesh=mesh, in_specs=in_specs, out_specs=P(None, "pb", None), check_vma=False
    )
```
